256 devices in a mesh: seq: 64 (over y_hi, z, x), ch: 4 (over y_lo, core).
Axes of the slice: x: 4, y: 4 (y_hi: 2, y_lo: 2; y = y_hi * 2 + y_lo), z: 8, core: 2. Of those that a mesh axis runs over, the one named last changes fastest.
Arguments:
- query_raw: bfloat16 [8192, 2048], P('seq', 'ch'), may hold values from -6 to 6
- key_raw: bfloat16 [8192, 2048], P('seq', 'ch'), may hold values from -6 to 6
- value_raw: bfloat16 [8192, 2048], P('seq', 'ch'), may hold values from -6 to 6
- featurizer: float32 [3, 7, 2048], P(None, None, 'ch'), may hold values from -2 to 2
- filter_taps: bfloat16 [8192, 2048], P(('seq', 'ch')), may hold values from -2.5 to 2.5
- cotangent: bfloat16 [8192, 2048], P('seq', 'ch'), may hold values from -6 to 6
Outputs:
- mixed: bfloat16 [8192, 2048], P('seq', 'ch')
- query_grad: bfloat16 [8192, 2048], P('seq', 'ch')
- key_grad: bfloat16 [8192, 2048], P('seq', 'ch')
- value_grad: bfloat16 [8192, 2048], P('seq', 'ch')
- filter_grad: float32 [8192, 2048], P(('seq', 'ch'))
- featurizer_grad: float32 [3, 7, 2048], P(None, None, 'ch')
The draws below stay inside these ranges and needn't reach their ends.
All inputs are finite; a program needn't handle non-finite values.
Results may differ from the reference program's by a relative error of at most 0.0085.
Values may be sent and summed in bfloat16 or wider, within the bound.
No kernel may reach another device: no remote copies, remote signals or barrier semaphores. Data moves between devices by JAX's collectives and lax.ppermute only.
A program may use at most 64 MiB of HBM per device.

```python
import math
import jax
import jax.numpy as jnp
from jax import lax

D = 2048
TAPS = 7
TOKENS = 8192


def draw_filter_taps(key, part):
    base = jax.random.fold_in(key, 7)
    noise_key, rate_key, pick_key, amp_key = jax.random.split(base, 4)
    positions = jnp.arange(TOKENS, dtype=jnp.float32)
    slow_rate = math.log(10.0) / TOKENS
    slow_rates = slow_rate * jnp.exp(jax.random.uniform(rate_key, (D,), jnp.float32, math.log(0.25), 0.0))
    fast_rates = jnp.exp(jax.random.uniform(jax.random.fold_in(rate_key, 3), (D,), jnp.float32, math.log(1.0 / 50.0), math.log(1.0 / 30.0)))
    picked = jax.random.bernoulli(pick_key, 0.5, (D,))
    rates = jnp.where(picked, slow_rates, fast_rates)
    noise = jax.random.truncated_normal(noise_key, -4.0, 4.0, (TOKENS, D), jnp.float32)
    amplitude = jnp.sqrt((1.0 - jnp.exp(-2.0 * rates)) / (1.0 - jnp.exp(-2.0 * rates * TOKENS)))
    amplitude = amplitude * jnp.exp(jax.random.uniform(amp_key, (D,), jnp.float32, math.log(0.5), math.log(2.0)))
    taps = noise * amplitude[None, :] * jnp.exp(-rates[None, :] * positions[:, None])
    return taps.astype(jnp.bfloat16)


def levels(own_key, shape, pieces, least, top_value):
    factor_of = 1.0
    for dim, shards_of in pieces:
        draws = jax.random.uniform(jax.random.fold_in(jax.random.fold_in(own_key, 6), dim), (shards_of,), jnp.float32, least / len(pieces), top_value / len(pieces))
        factor_of = factor_of * jnp.repeat(jnp.exp(draws), shape[dim] // shards_of).reshape((-1,) + (1,) * (len(shape) - 1 - dim))
    return factor_of


def normal_values(own_key, dims, spread, bound, cuts=(), kind=jnp.bfloat16):
    entries = spread * jax.random.normal(own_key, dims, jnp.float32)
    if cuts:
        entries = entries * levels(own_key, dims, cuts, -0.22, 0.18)
    return jnp.clip(entries, -bound, bound).astype(kind)


def setup_inputs(seed: int = 0) -> dict:
    splits = jax.random.split(jax.random.key(seed), 7)
    query_raw = normal_values(splits[0], (TOKENS, D), 1.0, 6.0, ((0, 64), (1, 4)))
    key_raw = normal_values(splits[1], (TOKENS, D), 1.0, 6.0, ((0, 64), (1, 4)))
    value_raw = normal_values(splits[2], (TOKENS, D), 1.0, 6.0, ((0, 64), (1, 4)))
    featurizer = normal_values(splits[3], (3, TAPS, D), TAPS ** -0.5, 2.0, ((2, 4),), jnp.float32)
    filter_taps = draw_filter_taps(jax.random.fold_in(splits[6], 71), 0)
    cotangent = normal_values(splits[5], (TOKENS, D), 1.0, 6.0, ((0, 64), (1, 4)))
    return {"query_raw": query_raw, "key_raw": key_raw, "value_raw": value_raw, "featurizer": featurizer, "filter_taps": filter_taps, "cotangent": cotangent}


def featurize(raw, weight):
    signal = raw.astype(jnp.float32)
    padded = jnp.pad(signal, ((TAPS - 1, 0), (0, 0)))
    total = jnp.zeros_like(signal)
    for lag_index in range(TAPS):
        start = TAPS - 1 - lag_index
        total = total + weight[lag_index][None, :] * padded[start:start + TOKENS]
    return total


def unfeaturize(grad, weight):
    padded = jnp.pad(grad, ((0, TAPS - 1), (0, 0)))
    total = jnp.zeros_like(grad)
    for lag_index in range(TAPS):
        total = total + weight[lag_index][None, :] * padded[lag_index:lag_index + TOKENS]
    return total


def weight_terms(grad, raw):
    padded = jnp.pad(raw.astype(jnp.float32), ((TAPS - 1, 0), (0, 0)))
    terms = []
    for lag_index in range(TAPS):
        start = TAPS - 1 - lag_index
        terms.append(jnp.sum(grad * padded[start:start + TOKENS], axis=0))
    return jnp.stack(terms)


def reference(query_raw, key_raw, value_raw, featurizer, filter_taps, cotangent):
    feat_query = featurize(query_raw, featurizer[0])
    feat_key = featurize(key_raw, featurizer[1])
    feat_value = featurize(value_raw, featurizer[2])
    mixer = (feat_key * feat_value).astype(jnp.bfloat16)
    upstream = cotangent.astype(jnp.float32)
    gate = (upstream * feat_query).astype(jnp.bfloat16)
    block_width = math.gcd(D, 256)
    full_len = 2 * TOKENS

    def to_blocks(array):
        return array.astype(jnp.float32).T.reshape(D // block_width, block_width, TOKENS)

    def from_blocks(array):
        return array.reshape(D, TOKENS).T

    def per_block(items):
        mix_block, taps_block, gate_block = items
        mix_spec = jnp.fft.rfft(mix_block, n=full_len, axis=-1)
        taps_spec = jnp.fft.rfft(taps_block, n=full_len, axis=-1)
        gate_spec = jnp.fft.rfft(gate_block, n=full_len, axis=-1)
        conv_block = jnp.fft.irfft(taps_spec * mix_spec, n=full_len, axis=-1)[:, :TOKENS]
        mix_grad_block = jnp.fft.irfft(jnp.conj(taps_spec) * gate_spec, n=full_len, axis=-1)[:, :TOKENS]
        taps_grad_block = jnp.fft.irfft(jnp.conj(mix_spec) * gate_spec, n=full_len, axis=-1)[:, :TOKENS]
        return conv_block, mix_grad_block, taps_grad_block

    conv, mixer_grad, taps_grad = lax.map(per_block, (to_blocks(mixer), to_blocks(filter_taps), to_blocks(gate)))
    scale = TOKENS ** -0.5
    conv = from_blocks(conv).astype(jnp.bfloat16)
    mixer_grad = from_blocks(mixer_grad).astype(jnp.bfloat16)
    filter_grad = from_blocks(taps_grad).astype(jnp.float32) * scale
    conv_float = conv.astype(jnp.float32)
    mixed = (feat_query * conv_float).astype(jnp.bfloat16)
    mix_grad_float = mixer_grad.astype(jnp.float32)
    query_feat_grad = upstream * conv_float
    key_feat_grad = mix_grad_float * feat_value
    value_feat_grad = mix_grad_float * feat_key
    query_grad = unfeaturize(query_feat_grad, featurizer[0]).astype(jnp.bfloat16)
    key_grad = unfeaturize(key_feat_grad, featurizer[1]).astype(jnp.bfloat16)
    value_grad = unfeaturize(value_feat_grad, featurizer[2]).astype(jnp.bfloat16)
    featurizer_grad = jnp.stack([
        weight_terms(query_feat_grad, query_raw),
        weight_terms(key_feat_grad, key_raw),
        weight_terms(value_feat_grad, value_raw),
    ]) * scale
    return mixed, query_grad, key_grad, value_grad, filter_grad, featurizer_grad
```

```python
import functools

import jax
import jax.numpy as jnp
from jax import lax
from jax.experimental import pallas as pl
from jax.experimental.pallas import tpu as pltpu
from jax.sharding import Mesh
from jax.sharding import PartitionSpec as P

TAPS = 7
SEQ = ("seq_0", "seq_1", "seq_2")
SEQ_CH = ("seq_0", "seq_1", "seq_2", "ch")
LANES = 128
OWN = 8
VMEM_LIMIT = 56 * 1024 * 1024

f32 = jnp.float32
bf16 = jnp.bfloat16


def pack_kernel(q_ref, k_ref, v_ref, c_ref, h_ref, out_ref):
    for index, ref in enumerate((q_ref, k_ref, v_ref, c_ref, h_ref)):
        turned = ref[...].astype(f32).T
        blocks = turned.reshape(turned.shape[0] // OWN, OWN, LANES)
        out_ref[:, index * OWN : (index + 1) * OWN, :] = blocks.astype(bf16)


def unpack_kernel(in_ref, mixed_ref, qg_ref, kg_ref, vg_ref, fg_ref, wg_ref):
    for index, ref in enumerate((mixed_ref, qg_ref, kg_ref, vg_ref, fg_ref)):
        blocks = in_ref[:, index * OWN : (index + 1) * OWN, :].astype(f32)
        rows = blocks.reshape(blocks.shape[0] * OWN, LANES)
        ref[...] = rows.T.astype(bf16)
    blocks = in_ref[:, 5 * OWN : 6 * OWN, :].astype(f32)
    sums = blocks.reshape(blocks.shape[0] * OWN, LANES).T
    wg_ref[...] = sums[0:24] + sums[32:56]


def backward_shifts(block, after_rolled, lane):
    rolled = [pltpu.roll(block, LANES - j, 1) for j in range(1, TAPS)]
    shifted = [
        jnp.where(lane < LANES - j, rolled[j - 1], after_rolled[j - 1]) for j in range(1, TAPS)
    ]
    return rolled, shifted


def owner_kernel(
    in_ref,
    w_ref,
    out_ref,
    fq_ref,
    fk_ref,
    fv_ref,
    mix_ref,
    gate_ref,
    tap_ref,
    xm_ref,
    xg_ref,
    xh_ref,
    res_ref,
    *,
    blocks,
    scale,
):
    lane = lax.broadcasted_iota(jnp.int32, (OWN, LANES), 1)
    flip_row = lax.broadcasted_iota(jnp.int32, (LANES, LANES), 0)
    flip_col = lax.broadcasted_iota(jnp.int32, (LANES, LANES), 1)
    flip = (flip_row + flip_col == LANES - 1).astype(f32).astype(bf16)
    zero = jnp.zeros((OWN, LANES), f32)

    def slab(s, index):
        return in_ref[s, index * OWN : (index + 1) * OWN, :].astype(f32)

    def forward(s, carry):
        feats = []
        after = []
        for index in range(3):
            block = slab(s, index)
            rolled = [pltpu.roll(block, j, 1) for j in range(1, TAPS)]
            total = w_ref[index * TAPS] * block
            for j in range(1, TAPS):
                shifted = jnp.where(lane >= j, rolled[j - 1], carry[index * (TAPS - 1) + j - 1])
                total = total + w_ref[index * TAPS + j] * shifted
            after += rolled
            feats.append(total)
        fq_ref[s], fk_ref[s], fv_ref[s] = feats
        rows = pl.ds(pl.multiple_of(s * OWN, OWN), OWN)
        mix_ref[rows, :] = (feats[1] * feats[2]).astype(bf16).astype(f32)
        gate_ref[rows, :] = (slab(s, 3) * feats[0]).astype(bf16).astype(f32)
        tap_ref[rows, :] = slab(s, 4)
        return tuple(after)

    lax.fori_loop(0, blocks, forward, (zero,) * (3 * (TAPS - 1)), unroll=2)

    res_ref[...] = jnp.dot(gate_ref[...].astype(bf16), flip, preferred_element_type=f32)

    @pl.loop(0, blocks)
    def _(s):
        rows = pl.ds(pl.multiple_of(s * OWN, OWN), OWN)
        back = pl.ds(pl.multiple_of((blocks - 1 - s) * OWN, OWN), OWN)
        gate_ref[rows, :] = res_ref[back, :]

    for r in range(OWN):
        for source, target in ((mix_ref, xm_ref), (gate_ref, xg_ref), (tap_ref, xh_ref)):
            target[r, :blocks, :] = jnp.zeros((blocks, LANES), f32)
            target[r, blocks:, :] = source[pl.ds(r, blocks, stride=OWN), :]

    wide_row = lax.broadcasted_iota(jnp.int32, (LANES, LANES), 0)
    wide_col = lax.broadcasted_iota(jnp.int32, (LANES, LANES), 1)
    causal = wide_col >= wide_row

    def long_conv(r, toeplitz_ref, operand_refs):
        before = jnp.zeros((LANES, LANES), f32)
        totals = [[None] * (blocks // 16) for _ in operand_refs]
        for pair in range(blocks // 2):
            tiles = []
            for d in (2 * pair, 2 * pair + 1):
                row = toeplitz_ref[r, blocks + d : blocks + d + 1, :]
                turned = pltpu.roll(
                    jnp.broadcast_to(row, (LANES, LANES)), 0, 1, stride=1, stride_axis=0
                )
                tiles.append(jnp.where(causal, turned, before).astype(bf16))
                before = turned
            right = jnp.concatenate(tiles, axis=0)
            first = (2 * pair) // 16
            for o, operand_ref in enumerate(operand_refs):
                left = jnp.concatenate(
                    [
                        operand_ref[r, blocks - d + 16 * first : 2 * blocks - d, :].astype(bf16)
                        for d in (2 * pair, 2 * pair + 1)
                    ],
                    axis=1,
                )
                product = jnp.dot(left, right, preferred_element_type=f32)
                for part in range(first, blocks // 16):
                    piece = product[16 * (part - first) : 16 * (part - first + 1)]
                    old = totals[o][part]
                    totals[o][part] = piece if old is None else old + piece
        return [jnp.concatenate(parts, axis=0) for parts in totals]

    @pl.loop(0, OWN)
    def _(r):
        (taps_sum,) = long_conv(r, xm_ref, (xg_ref,))
        tap_ref[pl.ds(r, blocks, stride=OWN), :] = taps_sum * scale

    @pl.loop(0, OWN)
    def _(r):
        conv, mix_grad = long_conv(r, xh_ref, (xm_ref, xg_ref))
        mix_ref[pl.ds(r, blocks, stride=OWN), :] = conv
        gate_ref[pl.ds(r, blocks, stride=OWN), :] = mix_grad

    res_ref[...] = jnp.dot(gate_ref[...].astype(bf16), flip, preferred_element_type=f32)
    gate_ref[...] = jnp.dot(tap_ref[...].astype(bf16), flip, preferred_element_type=f32)

    def backward(step, carry):
        s = blocks - 1 - step
        rows = pl.ds(pl.multiple_of(s * OWN, OWN), OWN)
        back = pl.ds(pl.multiple_of(step * OWN, OWN), OWN)
        conv = mix_ref[rows, :].astype(bf16).astype(f32)
        mix_grad = res_ref[back, :]
        upstream = slab(s, 3)
        grads = (upstream * conv, mix_grad * fv_ref[s], mix_grad * fk_ref[s])
        after, sums = carry
        new_after, new_sums = [], []
        outs = [fq_ref[s] * conv]
        for index in range(3):
            raw = slab(s, index)
            kept = after[index * (TAPS - 1) : (index + 1) * (TAPS - 1)]
            rolled, shifted = backward_shifts(grads[index], kept, lane)
            new_after += rolled
            total = w_ref[index * TAPS] * grads[index]
            new_sums.append(sums[index * TAPS] + raw * grads[index])
            for j in range(1, TAPS):
                total = total + w_ref[index * TAPS + j] * shifted[j - 1]
                new_sums.append(sums[index * TAPS + j] + raw * shifted[j - 1])
            outs.append(total)
        outs.append(gate_ref[back, :])
        for index, value in enumerate(outs):
            out_ref[s, index * OWN : (index + 1) * OWN, :] = value.astype(bf16)
        return tuple(new_after), tuple(new_sums)

    _, sums = lax.fori_loop(
        0, blocks, backward, ((zero,) * (3 * (TAPS - 1)), (zero,) * (3 * TAPS))
    )
    high = zero
    low = zero
    for index, value in enumerate(sums):
        total = jnp.sum(value, axis=1, keepdims=True) * scale
        coarse = total.astype(bf16).astype(f32)
        high = jnp.where(lane == index, coarse, high)
        low = jnp.where(lane == index + 32, total - coarse, low)
    packed = (high + low).astype(bf16)

    @pl.loop(0, blocks)
    def _(s):
        out_ref[s, 5 * OWN : 6 * OWN, :] = packed


def on_device(query_raw, key_raw, value_raw, featurizer, filter_taps, cotangent):
    tok_rows, channels = query_raw.shape
    seq_size = lax.axis_size(SEQ)
    ch_size = lax.axis_size("ch")
    me = lax.axis_index(SEQ)
    params = pltpu.CompilerParams(vmem_limit_bytes=VMEM_LIMIT)

    sub_rows = filter_taps.shape[0]
    taps_split = filter_taps.reshape(sub_rows, ch_size, channels).transpose(1, 0, 2)
    taps_rows = lax.all_to_all(taps_split, "ch", split_axis=0, concat_axis=0, tiled=True)
    taps_rows = taps_rows.reshape(tok_rows, channels)

    packed = pl.pallas_call(
        pack_kernel,
        out_shape=jax.ShapeDtypeStruct((seq_size, 5 * OWN, LANES), bf16),
        compiler_params=params,
        name="pack",
    )(query_raw, key_raw, value_raw, cotangent, taps_rows)
    received = lax.all_to_all(packed, SEQ, split_axis=0, concat_axis=0, tiled=True)

    own = lax.dynamic_slice(featurizer, (0, 0, me * OWN), (3, TAPS, OWN))
    own = jnp.broadcast_to(own.reshape(3 * TAPS, OWN, 1), (3 * TAPS, OWN, LANES))
    rows = seq_size * OWN
    flat = pltpu.VMEM((rows, LANES), f32)
    by_block = pltpu.VMEM((seq_size, OWN, LANES), f32)
    by_channel = pltpu.VMEM((OWN, 2 * seq_size, LANES), f32)
    outgoing = pl.pallas_call(
        functools.partial(owner_kernel, blocks=seq_size, scale=(seq_size * LANES) ** -0.5),
        out_shape=jax.ShapeDtypeStruct((seq_size, 6 * OWN, LANES), bf16),
        scratch_shapes=[by_block] * 3 + [flat] * 3 + [by_channel] * 3 + [flat],
        compiler_params=params,
        name="owner",
    )(received, own)
    returned = lax.all_to_all(outgoing, SEQ, split_axis=0, concat_axis=0, tiled=True)

    here = jax.ShapeDtypeStruct((tok_rows, channels), bf16)
    mixed, query_grad, key_grad, value_grad, taps_grad, weight_sums = pl.pallas_call(
        unpack_kernel,
        out_shape=(here,) * 5 + (jax.ShapeDtypeStruct((24, channels), f32),),
        compiler_params=params,
        name="unpack",
    )(returned)
    filter_grad = lax.all_to_all(
        taps_grad.reshape(ch_size, sub_rows, channels), "ch", split_axis=0, concat_axis=0, tiled=True
    )
    filter_grad = filter_grad.transpose(1, 0, 2).reshape(sub_rows, ch_size * channels).astype(f32)
    featurizer_grad = weight_sums[: 3 * TAPS].reshape(3, TAPS, channels)
    return mixed, query_grad, key_grad, value_grad, filter_grad, featurizer_grad


def solution(mesh):
    finer = Mesh(mesh.devices.reshape(2, 8, 4, mesh.shape["ch"]), ("seq_0", "seq_1", "seq_2", "ch"))
    placed = (
        P(SEQ, "ch"),
        P(SEQ, "ch"),
        P(SEQ, "ch"),
        P(None, None, "ch"),
        P(SEQ_CH, None),
        P(SEQ, "ch"),
    )
    return jax.shard_map(
        on_device,
        mesh=finer,
        in_specs=placed,
        out_specs=(
            P(SEQ, "ch"),
            P(SEQ, "ch"),
            P(SEQ, "ch"),
            P(SEQ, "ch"),
            P(SEQ_CH, None),
            P(None, None, "ch"),
        ),
        check_vma=False,
    )
```

```python
import functools

import jax
import jax.numpy as jnp
from jax import lax
from jax.experimental import pallas as pl
from jax.experimental.pallas import tpu as pltpu
from jax.sharding import Mesh
from jax.sharding import PartitionSpec as P

TAPS = 7
SEQ = ("seq_0", "seq_1", "seq_2")
SEQ_CH = ("seq_0", "seq_1", "seq_2", "ch")
LANES = 128
OWN = 8
MIB = 1024 * 1024

f32 = jnp.float32
bf16 = jnp.bfloat16


def pack_kernel(q_ref, k_ref, v_ref, c_ref, h_ref, out_ref):
    for index, ref in enumerate((q_ref, k_ref, v_ref, c_ref, h_ref)):
        turned = ref[...].astype(f32).T
        blocks = turned.reshape(turned.shape[0] // OWN, OWN, LANES)
        out_ref[:, index * OWN : (index + 1) * OWN, :] = blocks.astype(bf16)


def unpack_kernel(in_ref, mixed_ref, qg_ref, kg_ref, vg_ref, fg_ref, wg_ref):
    for index, ref in enumerate((mixed_ref, qg_ref, kg_ref, vg_ref, fg_ref)):
        blocks = in_ref[:, index * OWN : (index + 1) * OWN, :].astype(f32)
        rows = blocks.reshape(blocks.shape[0] * OWN, LANES)
        ref[...] = rows.T.astype(bf16)
    blocks = in_ref[:, 5 * OWN : 6 * OWN, :].astype(f32)
    sums = blocks.reshape(blocks.shape[0] * OWN, LANES).T
    wg_ref[...] = sums[0:24] + sums[32:56]


def backward_shifts(block, after_rolled, lane):
    rolled = [pltpu.roll(block, LANES - j, 1) for j in range(1, TAPS)]
    shifted = [
        jnp.where(lane < LANES - j, rolled[j - 1], after_rolled[j - 1]) for j in range(1, TAPS)
    ]
    return rolled, shifted


def owner_kernel(
    in_ref,
    w_ref,
    out_ref,
    fq_ref,
    fk_ref,
    fv_ref,
    mix_ref,
    gate_ref,
    tap_ref,
    xm_ref,
    xg_ref,
    xh_ref,
    res_ref,
    *,
    blocks,
    scale,
):
    lane = lax.broadcasted_iota(jnp.int32, (OWN, LANES), 1)
    flip_row = lax.broadcasted_iota(jnp.int32, (LANES, LANES), 0)
    flip_col = lax.broadcasted_iota(jnp.int32, (LANES, LANES), 1)
    flip = (flip_row + flip_col == LANES - 1).astype(f32).astype(bf16)
    zero = jnp.zeros((OWN, LANES), f32)

    def slab(s, index):
        return in_ref[s, index * OWN : (index + 1) * OWN, :].astype(f32)

    def forward(s, carry):
        feats = []
        after = []
        for index in range(3):
            block = slab(s, index)
            rolled = [pltpu.roll(block, j, 1) for j in range(1, TAPS)]
            total = w_ref[index * TAPS] * block
            for j in range(1, TAPS):
                shifted = jnp.where(lane >= j, rolled[j - 1], carry[index * (TAPS - 1) + j - 1])
                total = total + w_ref[index * TAPS + j] * shifted
            after += rolled
            feats.append(total)
        fq_ref[s], fk_ref[s], fv_ref[s] = feats
        rows = pl.ds(pl.multiple_of(s * OWN, OWN), OWN)
        mix_ref[rows, :] = (feats[1] * feats[2]).astype(bf16).astype(f32)
        gate_ref[rows, :] = (slab(s, 3) * feats[0]).astype(bf16).astype(f32)
        tap_ref[rows, :] = slab(s, 4)
        return tuple(after)

    lax.fori_loop(0, blocks, forward, (zero,) * (3 * (TAPS - 1)), unroll=2)

    res_ref[...] = jnp.dot(gate_ref[...].astype(bf16), flip, preferred_element_type=f32)

    @pl.loop(0, blocks)
    def _(s):
        rows = pl.ds(pl.multiple_of(s * OWN, OWN), OWN)
        back = pl.ds(pl.multiple_of((blocks - 1 - s) * OWN, OWN), OWN)
        gate_ref[rows, :] = res_ref[back, :]

    for r in range(OWN):
        for source, target in ((mix_ref, xm_ref), (gate_ref, xg_ref), (tap_ref, xh_ref)):
            target[r, :blocks, :] = jnp.zeros((blocks, LANES), f32)
            target[r, blocks:, :] = source[pl.ds(r, blocks, stride=OWN), :]

    wide_row = lax.broadcasted_iota(jnp.int32, (LANES, LANES), 0)
    wide_col = lax.broadcasted_iota(jnp.int32, (LANES, LANES), 1)
    causal = wide_col >= wide_row

    def long_conv(r, toeplitz_ref, operand_refs):
        before = jnp.zeros((LANES, LANES), f32)
        totals = [[None] * (blocks // 16) for _ in operand_refs]
        for pair in range(blocks // 2):
            tiles = []
            for d in (2 * pair, 2 * pair + 1):
                row = toeplitz_ref[r, blocks + d : blocks + d + 1, :]
                turned = pltpu.roll(
                    jnp.broadcast_to(row, (LANES, LANES)), 0, 1, stride=1, stride_axis=0
                )
                tiles.append(jnp.where(causal, turned, before).astype(bf16))
                before = turned
            right = jnp.concatenate(tiles, axis=0)
            first = (2 * pair) // 16
            for o, operand_ref in enumerate(operand_refs):
                left = jnp.concatenate(
                    [
                        operand_ref[r, blocks - d + 16 * first : 2 * blocks - d, :].astype(bf16)
                        for d in (2 * pair, 2 * pair + 1)
                    ],
                    axis=1,
                )
                product = jnp.dot(left, right, preferred_element_type=f32)
                for part in range(first, blocks // 16):
                    piece = product[16 * (part - first) : 16 * (part - first + 1)]
                    old = totals[o][part]
                    totals[o][part] = piece if old is None else old + piece
        return [jnp.concatenate(parts, axis=0) for parts in totals]

    @pl.loop(0, OWN)
    def _(r):
        (taps_sum,) = long_conv(r, xm_ref, (xg_ref,))
        tap_ref[pl.ds(r, blocks, stride=OWN), :] = taps_sum * scale

    @pl.loop(0, OWN)
    def _(r):
        conv, mix_grad = long_conv(r, xh_ref, (xm_ref, xg_ref))
        mix_ref[pl.ds(r, blocks, stride=OWN), :] = conv
        gate_ref[pl.ds(r, blocks, stride=OWN), :] = mix_grad

    res_ref[...] = jnp.dot(gate_ref[...].astype(bf16), flip, preferred_element_type=f32)
    gate_ref[...] = jnp.dot(tap_ref[...].astype(bf16), flip, preferred_element_type=f32)

    def backward(step, carry):
        s = blocks - 1 - step
        rows = pl.ds(pl.multiple_of(s * OWN, OWN), OWN)
        back = pl.ds(pl.multiple_of(step * OWN, OWN), OWN)
        conv = mix_ref[rows, :].astype(bf16).astype(f32)
        mix_grad = res_ref[back, :]
        upstream = slab(s, 3)
        grads = (upstream * conv, mix_grad * fv_ref[s], mix_grad * fk_ref[s])
        after, sums = carry
        new_after, new_sums = [], []
        outs = [fq_ref[s] * conv]
        for index in range(3):
            raw = slab(s, index)
            kept = after[index * (TAPS - 1) : (index + 1) * (TAPS - 1)]
            rolled, shifted = backward_shifts(grads[index], kept, lane)
            new_after += rolled
            total = w_ref[index * TAPS] * grads[index]
            new_sums.append(sums[index * TAPS] + raw * grads[index])
            for j in range(1, TAPS):
                total = total + w_ref[index * TAPS + j] * shifted[j - 1]
                new_sums.append(sums[index * TAPS + j] + raw * shifted[j - 1])
            outs.append(total)
        outs.append(gate_ref[back, :])
        for index, value in enumerate(outs):
            out_ref[s, index * OWN : (index + 1) * OWN, :] = value.astype(bf16)
        return tuple(new_after), tuple(new_sums)

    _, sums = lax.fori_loop(
        0, blocks, backward, ((zero,) * (3 * (TAPS - 1)), (zero,) * (3 * TAPS))
    )
    high = zero
    low = zero
    for index, value in enumerate(sums):
        total = jnp.sum(value, axis=1, keepdims=True) * scale
        coarse = total.astype(bf16).astype(f32)
        high = jnp.where(lane == index, coarse, high)
        low = jnp.where(lane == index + 32, total - coarse, low)
    packed = (high + low).astype(bf16)

    @pl.loop(0, blocks)
    def _(s):
        out_ref[s, 5 * OWN : 6 * OWN, :] = packed


def on_device(query_raw, key_raw, value_raw, featurizer, filter_taps, cotangent):
    tok_rows, channels = query_raw.shape
    seq_size = lax.axis_size(SEQ)
    ch_size = lax.axis_size("ch")
    me = lax.axis_index(SEQ)
    small = pltpu.CompilerParams(vmem_limit_bytes=8 * MIB)
    large = pltpu.CompilerParams(vmem_limit_bytes=16 * MIB)

    sub_rows = filter_taps.shape[0]
    taps_split = filter_taps.reshape(sub_rows, ch_size, channels).transpose(1, 0, 2)
    taps_rows = lax.all_to_all(taps_split, "ch", split_axis=0, concat_axis=0, tiled=True)
    taps_rows = taps_rows.reshape(tok_rows, channels)

    packed = pl.pallas_call(
        pack_kernel,
        out_shape=jax.ShapeDtypeStruct((seq_size, 5 * OWN, LANES), bf16),
        compiler_params=small,
        name="pack",
    )(query_raw, key_raw, value_raw, cotangent, taps_rows)
    own = lax.dynamic_slice(featurizer, (0, 0, me * OWN), (3, TAPS, OWN))
    own = jnp.broadcast_to(own.reshape(3 * TAPS, OWN, 1), (3 * TAPS, OWN, LANES))
    packed, own = lax.optimization_barrier((packed, own))
    received = lax.all_to_all(packed, SEQ, split_axis=0, concat_axis=0, tiled=True)
    rows = seq_size * OWN
    flat = pltpu.VMEM((rows, LANES), f32)
    by_block = pltpu.VMEM((seq_size, OWN, LANES), f32)
    by_channel = pltpu.VMEM((OWN, 2 * seq_size, LANES), f32)
    outgoing = pl.pallas_call(
        functools.partial(owner_kernel, blocks=seq_size, scale=(seq_size * LANES) ** -0.5),
        out_shape=jax.ShapeDtypeStruct((seq_size, 6 * OWN, LANES), bf16),
        scratch_shapes=[by_block] * 3 + [flat] * 3 + [by_channel] * 3 + [flat],
        compiler_params=large,
        name="owner",
    )(received, own)
    returned = lax.all_to_all(outgoing, SEQ, split_axis=0, concat_axis=0, tiled=True)

    here = jax.ShapeDtypeStruct((tok_rows, channels), bf16)
    mixed, query_grad, key_grad, value_grad, taps_grad, weight_sums = pl.pallas_call(
        unpack_kernel,
        out_shape=(here,) * 5 + (jax.ShapeDtypeStruct((24, channels), f32),),
        compiler_params=small,
        name="unpack",
    )(returned)
    filter_grad = lax.all_to_all(
        taps_grad.reshape(ch_size, sub_rows, channels), "ch", split_axis=0, concat_axis=0, tiled=True
    )
    filter_grad = filter_grad.transpose(1, 0, 2).reshape(sub_rows, ch_size * channels).astype(f32)
    featurizer_grad = weight_sums[: 3 * TAPS].reshape(3, TAPS, channels)
    return mixed, query_grad, key_grad, value_grad, filter_grad, featurizer_grad


def solution(mesh):
    finer = Mesh(mesh.devices.reshape(2, 8, 4, mesh.shape["ch"]), ("seq_0", "seq_1", "seq_2", "ch"))
    placed = (
        P(SEQ, "ch"),
        P(SEQ, "ch"),
        P(SEQ, "ch"),
        P(None, None, "ch"),
        P(SEQ_CH, None),
        P(SEQ, "ch"),
    )
    return jax.shard_map(
        on_device,
        mesh=finer,
        in_specs=placed,
        out_specs=(
            P(SEQ, "ch"),
            P(SEQ, "ch"),
            P(SEQ, "ch"),
            P(SEQ, "ch"),
            P(SEQ_CH, None),
            P(None, None, "ch"),
        ),
        check_vma=False,
    )
```

```python
import functools

import jax
import jax.numpy as jnp
from jax import lax
from jax.experimental import pallas as pl
from jax.experimental.pallas import tpu as pltpu
from jax.sharding import Mesh
from jax.sharding import PartitionSpec as P

TAPS = 7
SEQ = ("seq_0", "seq_1", "seq_2")
SEQ_CH = ("seq_0", "seq_1", "seq_2", "ch")
LANES = 128
OWN = 8
GROUPS = 4
PIECE = LANES // GROUPS
WIDTH = 11 * LANES
MIB = 1024 * 1024

f32 = jnp.float32
bf16 = jnp.bfloat16


def pack_kernel(q_ref, k_ref, v_ref, c_ref, h_ref, w_ref, out_ref, weight_ref):
    half = out_ref.shape[0]
    rows = [ref[...].astype(f32) for ref in (q_ref, k_ref, v_ref, c_ref)]
    taps = h_ref[...].astype(f32)
    wide = 2 * half
    rows.append(jnp.concatenate([taps[:, g * wide : (g + 1) * wide] for g in range(GROUPS)], axis=0))
    for index, value in enumerate(rows):
        turned = value.T.astype(bf16)
        for e in range(2):
            column = (2 * index + e) * LANES
            out_ref[:, column : column + LANES] = turned[e * half : (e + 1) * half]
    weight_ref[...] = jnp.zeros_like(weight_ref)
    for index in range(3):
        weight = w_ref[index]
        coarse = weight.astype(bf16).astype(f32)
        for e in range(2):
            part = slice(e * half, (e + 1) * half)
            row = 64 * e + TAPS * index
            weight_ref[row : row + TAPS, :] = coarse[:, part]
            weight_ref[row + 32 : row + 32 + TAPS, :] = (weight - coarse)[:, part]
    out_ref[:, 10 * LANES :] = weight_ref[...].T.astype(bf16)


def unpack_kernel(in_ref, mixed_ref, qg_ref, kg_ref, vg_ref, fg_ref, wg_ref):
    half = in_ref.shape[0]

    def turned(index, e):
        column = (2 * index + e) * LANES
        return in_ref[:, column : column + LANES].astype(f32).T

    for e in range(2):
        part = slice(e * half, (e + 1) * half)
        for index, ref in enumerate((mixed_ref, qg_ref, kg_ref, vg_ref)):
            ref[:, part] = turned(index, e).astype(bf16)
        taps_grad = turned(4, e)
        for g in range(GROUPS):
            column = g * 2 * half + e * half
            fg_ref[:, column : column + half] = taps_grad[g * PIECE : (g + 1) * PIECE]
    sums = in_ref[:, 10 * LANES :].astype(f32).T
    for e in range(2):
        part = slice(e * half, (e + 1) * half)
        total = sums[64 * e : 64 * e + 24] + sums[64 * e + 32 : 64 * e + 56]
        for index in range(3):
            wg_ref[index, :, part] = total[TAPS * index : TAPS * (index + 1)]


def owner_kernel(
    in_ref,
    out_ref,
    w_ref,
    raw_ref,
    feat_ref,
    mix_ref,
    gate_ref,
    tap_ref,
    xm_ref,
    xg_ref,
    xh_ref,
    res_ref,
    *,
    blocks,
    scale,
):
    lane = lax.broadcasted_iota(jnp.int32, (OWN, LANES), 1)
    row = lax.broadcasted_iota(jnp.int32, (OWN, LANES), 0)
    first_half = row < GROUPS
    group = row % GROUPS
    piece = lane // PIECE
    flip_row = lax.broadcasted_iota(jnp.int32, (LANES, LANES), 0)
    flip_col = lax.broadcasted_iota(jnp.int32, (LANES, LANES), 1)
    flip = (flip_row + flip_col == LANES - 1).astype(f32).astype(bf16)
    zero = jnp.zeros((OWN, LANES), f32)
    steps = blocks // 4

    def half_turn(value):
        return pltpu.roll(value, GROUPS, 0)

    def regroup(one, two):
        return (
            jnp.where(first_half, one, half_turn(two)),
            jnp.where(first_half, half_turn(one), two),
        )

    def swap_pieces(value):
        result = value
        for k in range(1, GROUPS):
            moved = pltpu.roll(value, PIECE * k, 1)
            up = pltpu.roll(moved, OWN - k, 0)
            down = pltpu.roll(moved, GROUPS - k, 0)
            taken = jnp.where(group + k < GROUPS, up, down)
            result = jnp.where(piece == (group + k) % GROUPS, taken, result)
        return result

    def block_rows(s):
        return pl.ds(pl.multiple_of(s * OWN, OWN), OWN)

    weights = in_ref[0:OWN, 10 * LANES :].astype(f32)
    weights = jnp.where(first_half, weights, pltpu.roll(weights, 64, 1))
    weights = weights + pltpu.roll(weights, LANES - 32, 1)
    for index in range(3 * TAPS):
        w_ref[index] = jnp.broadcast_to(weights[:, index : index + 1], (OWN, LANES))

    @pl.loop(0, steps)
    def _(step):
        rows = pl.ds(pl.multiple_of(step * 16, 16), 16)
        for index in range(5):
            one = in_ref[rows, 2 * index * LANES : (2 * index + 1) * LANES].astype(f32)
            two = in_ref[rows, (2 * index + 1) * LANES : (2 * index + 2) * LANES].astype(f32)
            for part in range(2):
                pair = regroup(one[part * OWN : (part + 1) * OWN], two[part * OWN : (part + 1) * OWN])
                for which, value in enumerate(pair):
                    s = step * 4 + part * 2 + which
                    if index < 4:
                        raw_ref[index, s] = value
                    else:
                        tap_ref[block_rows(s), :] = swap_pieces(value)

    for index in range(3):

        def forward(step, kept, index=index):
            for which in range(4):
                s = step * 4 + which
                block = raw_ref[index, s]
                rolled = tuple(pltpu.roll(block, j, 1) for j in range(1, TAPS))
                total = w_ref[index * TAPS] * block
                for j in range(1, TAPS):
                    shifted = jnp.where(lane >= j, rolled[j - 1], kept[j - 1])
                    total = total + w_ref[index * TAPS + j] * shifted
                kept = rolled
                feat_ref[index, s] = total
                if index == 0:
                    gate_ref[block_rows(s), :] = (raw_ref[3, s] * total).astype(bf16).astype(f32)
                if index == 2:
                    mix_ref[block_rows(s), :] = (feat_ref[1, s] * total).astype(bf16).astype(f32)
            return kept

        lax.fori_loop(0, steps, forward, (zero,) * (TAPS - 1))

    res_ref[...] = jnp.dot(gate_ref[...].astype(bf16), flip, preferred_element_type=f32)

    @pl.loop(0, blocks)
    def _(s):
        gate_ref[block_rows(s), :] = res_ref[block_rows(blocks - 1 - s), :]

    for r in range(OWN):
        for source, target in ((mix_ref, xm_ref), (gate_ref, xg_ref), (tap_ref, xh_ref)):
            target[r, :blocks, :] = jnp.zeros((blocks, LANES), f32)
            target[r, blocks:, :] = source[pl.ds(r, blocks, stride=OWN), :]

    causal = flip_col >= flip_row

    def long_conv(r, toeplitz_ref, operand_refs):
        before = jnp.zeros((LANES, LANES), f32)
        totals = [[None] * (blocks // 16) for _ in operand_refs]
        for pair in range(blocks // 2):
            tiles = []
            for d in (2 * pair, 2 * pair + 1):
                line = toeplitz_ref[r, blocks + d : blocks + d + 1, :]
                turned = pltpu.roll(
                    jnp.broadcast_to(line, (LANES, LANES)), 0, 1, stride=1, stride_axis=0
                )
                tiles.append(jnp.where(causal, turned, before).astype(bf16))
                before = turned
            right = jnp.concatenate(tiles, axis=0)
            first = (2 * pair) // 16
            for o, operand_ref in enumerate(operand_refs):
                left = jnp.concatenate(
                    [
                        operand_ref[r, blocks - d + 16 * first : 2 * blocks - d, :].astype(bf16)
                        for d in (2 * pair, 2 * pair + 1)
                    ],
                    axis=1,
                )
                product = jnp.dot(left, right, preferred_element_type=f32)
                for part in range(first, blocks // 16):
                    added = product[16 * (part - first) : 16 * (part - first + 1)]
                    old = totals[o][part]
                    totals[o][part] = added if old is None else old + added
        return [jnp.concatenate(parts, axis=0) for parts in totals]

    @pl.loop(0, OWN)
    def _(r):
        (taps_sum,) = long_conv(r, xm_ref, (xg_ref,))
        tap_ref[pl.ds(r, blocks, stride=OWN), :] = taps_sum * scale

    @pl.loop(0, OWN)
    def _(r):
        conv, mix_grad = long_conv(r, xh_ref, (xm_ref, xg_ref))
        mix_ref[pl.ds(r, blocks, stride=OWN), :] = conv
        gate_ref[pl.ds(r, blocks, stride=OWN), :] = mix_grad

    res_ref[...] = jnp.dot(gate_ref[...].astype(bf16), flip, preferred_element_type=f32)
    gate_ref[...] = jnp.dot(tap_ref[...].astype(bf16), flip, preferred_element_type=f32)

    def put(step, index, values):
        ones, twos = zip(regroup(values[0], values[1]), regroup(values[2], values[3]))
        rows = pl.ds(pl.multiple_of(step * 16, 16), 16)
        for e, halves in enumerate((ones, twos)):
            column = (2 * index + e) * LANES
            out_ref[rows, column : column + LANES] = jnp.concatenate(halves, axis=0).astype(bf16)

    def back_block(s):
        return block_rows(blocks - 1 - s)

    @pl.loop(0, steps)
    def _(step):
        mixed, taps_grad = [], []
        for which in range(4):
            s = step * 4 + which
            conv = mix_ref[block_rows(s), :].astype(bf16).astype(f32)
            mix_ref[block_rows(s), :] = conv
            mixed.append(feat_ref[0, s] * conv)
            taps_grad.append(swap_pieces(gate_ref[back_block(s), :]))
        put(step, 0, mixed)
        put(step, 4, taps_grad)

    all_sums = []
    for index in range(3):

        def backward(count, carry, index=index):
            step = steps - 1 - count
            kept, sums = carry
            grads = [None] * 4
            for which in (3, 2, 1, 0):
                s = step * 4 + which
                if index == 0:
                    grad = raw_ref[3, s] * mix_ref[block_rows(s), :]
                else:
                    grad = res_ref[back_block(s), :] * feat_ref[3 - index, s]
                raw = raw_ref[index, s]
                rolled = tuple(pltpu.roll(grad, LANES - j, 1) for j in range(1, TAPS))
                total = w_ref[index * TAPS] * grad
                new_sums = [sums[0] + raw * grad]
                for j in range(1, TAPS):
                    shifted = jnp.where(lane < LANES - j, rolled[j - 1], kept[j - 1])
                    total = total + w_ref[index * TAPS + j] * shifted
                    new_sums.append(sums[j] + raw * shifted)
                kept, sums = rolled, tuple(new_sums)
                grads[which] = total
            put(step, index + 1, grads)
            return kept, sums

        _, sums = lax.fori_loop(0, steps, backward, ((zero,) * (TAPS - 1), (zero,) * TAPS))
        all_sums += sums

    high = zero
    low = zero
    for index, value in enumerate(all_sums):
        total = jnp.sum(value, axis=1, keepdims=True) * scale
        coarse = total.astype(bf16).astype(f32)
        high = jnp.where(lane == index, coarse, high)
        low = jnp.where(lane == index + 32, total - coarse, low)
    both = high + low
    both = jnp.where(lane < 64, both, pltpu.roll(half_turn(both), 64, 1))
    both = jnp.where(first_half, both, half_turn(both))
    both = jnp.concatenate([both, both], axis=0).astype(bf16)

    @pl.loop(0, steps)
    def _(step):
        out_ref[pl.ds(pl.multiple_of(step * 16, 16), 16), 10 * LANES :] = both


def on_device(query_raw, key_raw, value_raw, featurizer, filter_taps, cotangent):
    tok_rows, channels = query_raw.shape
    blocks = lax.axis_size(SEQ)
    devices = lax.axis_size(SEQ_CH)
    small = pltpu.CompilerParams(vmem_limit_bytes=12 * MIB)
    large = pltpu.CompilerParams(vmem_limit_bytes=20 * MIB)
    sent = jax.ShapeDtypeStruct((devices, WIDTH), bf16)

    packed = pl.pallas_call(
        pack_kernel,
        out_shape=sent,
        scratch_shapes=[pltpu.VMEM((LANES, devices), f32)],
        compiler_params=small,
        name="pack",
    )(query_raw, key_raw, value_raw, cotangent, filter_taps, featurizer)
    received = lax.all_to_all(packed, SEQ_CH, split_axis=0, concat_axis=0, tiled=True)

    flat = pltpu.VMEM((blocks * OWN, LANES), f32)
    by_channel = pltpu.VMEM((OWN, 2 * blocks, LANES), f32)
    outgoing = pl.pallas_call(
        functools.partial(owner_kernel, blocks=blocks, scale=(blocks * LANES) ** -0.5),
        out_shape=sent,
        scratch_shapes=[
            pltpu.VMEM((3 * TAPS, OWN, LANES), f32),
            pltpu.VMEM((4, blocks, OWN, LANES), f32),
            pltpu.VMEM((3, blocks, OWN, LANES), f32),
            flat,
            flat,
            flat,
            by_channel,
            by_channel,
            by_channel,
            flat,
        ],
        compiler_params=large,
        name="owner",
    )(received)
    returned = lax.all_to_all(outgoing, SEQ_CH, split_axis=0, concat_axis=0, tiled=True)

    here = jax.ShapeDtypeStruct((tok_rows, channels), bf16)
    return pl.pallas_call(
        unpack_kernel,
        out_shape=(here,) * 4
        + (
            jax.ShapeDtypeStruct(filter_taps.shape, f32),
            jax.ShapeDtypeStruct(featurizer.shape, f32),
        ),
        compiler_params=small,
        name="unpack",
    )(returned)


def solution(mesh):
    finer = Mesh(mesh.devices.reshape(2, 8, 4, mesh.shape["ch"]), ("seq_0", "seq_1", "seq_2", "ch"))
    placed = (
        P(SEQ, "ch"),
        P(SEQ, "ch"),
        P(SEQ, "ch"),
        P(None, None, "ch"),
        P(SEQ_CH, None),
        P(SEQ, "ch"),
    )
    return jax.shard_map(
        on_device,
        mesh=finer,
        in_specs=placed,
        out_specs=(
            P(SEQ, "ch"),
            P(SEQ, "ch"),
            P(SEQ, "ch"),
            P(SEQ, "ch"),
            P(SEQ_CH, None),
            P(None, None, "ch"),
        ),
        check_vma=False,
    )
```

```python
import functools

import jax
import jax.numpy as jnp
from jax import lax
from jax.experimental import pallas as pl
from jax.experimental.pallas import tpu as pltpu
from jax.sharding import Mesh
from jax.sharding import PartitionSpec as P

TAPS = 7
SEQ = ("seq_0", "seq_1", "seq_2")
SEQ_CH = ("seq_0", "seq_1", "seq_2", "ch")
LANES = 128
OWN = 8
GROUPS = 4
PIECE = LANES // GROUPS
WIDTH = 6 * LANES
MIB = 1024 * 1024

f32 = jnp.float32
bf16 = jnp.bfloat16


def pack_kernel(*refs):
    sources, out_ref, copies = refs[:6], refs[6], refs[7:13]
    weight_ref, sems = refs[13:]
    moves = [
        pltpu.make_async_copy(source, copy, sems.at[index])
        for index, (source, copy) in enumerate(zip(sources, copies))
    ]
    for move in moves:
        move.start()
    pairs = (out_ref.shape[0], 2, LANES)
    wide = out_ref.shape[0] * 2

    def put(index, rows):
        out_ref[:, :, index * LANES : (index + 1) * LANES] = rows.T.astype(bf16).reshape(pairs)

    weight_ref[...] = jnp.zeros_like(weight_ref)
    for index in range(4):
        moves[index].wait()
        put(index, copies[index][...].astype(f32))
    moves[4].wait()
    taps = copies[4][...].astype(f32)
    put(4, jnp.concatenate([taps[:, g * wide : (g + 1) * wide] for g in range(GROUPS)], axis=0))
    moves[5].wait()
    for index in range(3):
        weight = copies[5][index]
        coarse = weight.astype(bf16).astype(f32)
        row = TAPS * index
        weight_ref[row : row + TAPS, :] = coarse
        weight_ref[row + 32 : row + 32 + TAPS, :] = weight - coarse
    put(5, weight_ref[...])


def unpack_kernel(in_ref, mixed_ref, qg_ref, kg_ref, vg_ref, fg_ref, wg_ref):
    wide = in_ref.shape[0] * 2

    def turned(index):
        rows = in_ref[:, :, index * LANES : (index + 1) * LANES].reshape(wide, LANES)
        return rows.astype(f32).T

    for index, ref in enumerate((mixed_ref, qg_ref, kg_ref, vg_ref)):
        ref[...] = turned(index).astype(bf16)
    taps_grad = turned(4)
    for g in range(GROUPS):
        fg_ref[:, g * wide : (g + 1) * wide] = taps_grad[g * PIECE : (g + 1) * PIECE]
    sums = turned(5)
    total = sums[0:24] + sums[32:56]
    for index in range(3):
        wg_ref[index] = total[TAPS * index : TAPS * (index + 1)]


def owner_kernel(
    in_ref,
    out_ref,
    w_ref,
    raw_ref,
    feat_ref,
    mix_ref,
    gate_ref,
    tap_ref,
    xm_ref,
    xg_ref,
    xh_ref,
    res_ref,
    *,
    blocks,
    scale,
):
    lane = lax.broadcasted_iota(jnp.int32, (OWN, LANES), 1)
    row = lax.broadcasted_iota(jnp.int32, (OWN, LANES), 0)
    group = row // 2
    piece = lane // PIECE
    flip_row = lax.broadcasted_iota(jnp.int32, (LANES, LANES), 0)
    flip_col = lax.broadcasted_iota(jnp.int32, (LANES, LANES), 1)
    flip = (flip_row + flip_col == LANES - 1).astype(f32).astype(bf16)
    zero = jnp.zeros((OWN, LANES), f32)
    steps = blocks // 4

    def swap_pieces(value):
        result = value
        for k in range(1, GROUPS):
            moved = pltpu.roll(pltpu.roll(value, PIECE * k, 1), OWN - 2 * k, 0)
            result = jnp.where(piece == (group + k) % GROUPS, moved, result)
        return result

    def block_rows(s):
        return pl.ds(pl.multiple_of(s * OWN, OWN), OWN)

    def taken(step, index):
        rows = in_ref[pl.ds(step * 16, 16), :, index * LANES : (index + 1) * LANES]
        return rows.reshape(4 * OWN, LANES).astype(f32)

    weights = taken(0, 5)[:OWN]
    weights = weights + pltpu.roll(weights, LANES - 32, 1)
    for index in range(3 * TAPS):
        w_ref[index] = jnp.broadcast_to(weights[:, index : index + 1], (OWN, LANES))

    @pl.loop(0, steps)
    def _(step):
        for index in range(5):
            values = taken(step, index)
            for which in range(4):
                s = step * 4 + which
                value = values[which * OWN : (which + 1) * OWN]
                if index < 4:
                    raw_ref[index, s] = value
                else:
                    tap_ref[block_rows(s), :] = swap_pieces(value)

    for index in range(3):

        def forward(step, kept, index=index):
            for which in range(4):
                s = step * 4 + which
                block = raw_ref[index, s]
                rolled = tuple(pltpu.roll(block, j, 1) for j in range(1, TAPS))
                total = w_ref[index * TAPS] * block
                for j in range(1, TAPS):
                    shifted = jnp.where(lane >= j, rolled[j - 1], kept[j - 1])
                    total = total + w_ref[index * TAPS + j] * shifted
                kept = rolled
                feat_ref[index, s] = total
                if index == 0:
                    gate_ref[block_rows(s), :] = (raw_ref[3, s] * total).astype(bf16).astype(f32)
                if index == 2:
                    mix_ref[block_rows(s), :] = (feat_ref[1, s] * total).astype(bf16).astype(f32)
            return kept

        lax.fori_loop(0, steps, forward, (zero,) * (TAPS - 1))

    res_ref[...] = jnp.dot(gate_ref[...].astype(bf16), flip, preferred_element_type=f32)

    @pl.loop(0, blocks)
    def _(s):
        gate_ref[block_rows(s), :] = res_ref[block_rows(blocks - 1 - s), :]

    for r in range(OWN):
        for source, target in ((mix_ref, xm_ref), (gate_ref, xg_ref), (tap_ref, xh_ref)):
            target[r, :blocks, :] = jnp.zeros((blocks, LANES), f32)
            target[r, blocks:, :] = source[pl.ds(r, blocks, stride=OWN), :]

    causal = flip_col >= flip_row

    def long_conv(r, toeplitz_ref, operand_refs):
        before = jnp.zeros((LANES, LANES), bf16)
        totals = [[None] * (blocks // 16) for _ in operand_refs]
        for pair in range(blocks // 2):
            tiles = []
            for d in (2 * pair, 2 * pair + 1):
                line = toeplitz_ref[r, blocks + d : blocks + d + 1, :].astype(bf16)
                turned = pltpu.roll(
                    jnp.broadcast_to(line, (LANES, LANES)), 0, 1, stride=1, stride_axis=0
                )
                tiles.append(jnp.where(causal, turned, before))
                before = turned
            right = jnp.concatenate(tiles, axis=0)
            first = (2 * pair) // 16
            for o, operand_ref in enumerate(operand_refs):
                left = jnp.concatenate(
                    [
                        operand_ref[r, blocks - d + 16 * first : 2 * blocks - d, :].astype(bf16)
                        for d in (2 * pair, 2 * pair + 1)
                    ],
                    axis=1,
                )
                product = jnp.dot(left, right, preferred_element_type=f32)
                for part in range(first, blocks // 16):
                    added = product[16 * (part - first) : 16 * (part - first + 1)]
                    old = totals[o][part]
                    totals[o][part] = added if old is None else old + added
        return [jnp.concatenate(parts, axis=0) for parts in totals]

    @pl.loop(0, OWN)
    def _(r):
        (taps_sum,) = long_conv(r, xm_ref, (xg_ref,))
        tap_ref[pl.ds(r, blocks, stride=OWN), :] = taps_sum * scale

    @pl.loop(0, OWN)
    def _(r):
        conv, mix_grad = long_conv(r, xh_ref, (xm_ref, xg_ref))
        mix_ref[pl.ds(r, blocks, stride=OWN), :] = conv
        gate_ref[pl.ds(r, blocks, stride=OWN), :] = mix_grad

    res_ref[...] = jnp.dot(gate_ref[...].astype(bf16), flip, preferred_element_type=f32)
    gate_ref[...] = jnp.dot(tap_ref[...].astype(bf16), flip, preferred_element_type=f32)

    def put(step, index, values):
        rows = jnp.concatenate(values, axis=0).astype(bf16).reshape(16, 2, LANES)
        out_ref[pl.ds(step * 16, 16), :, index * LANES : (index + 1) * LANES] = rows

    def back_block(s):
        return block_rows(blocks - 1 - s)

    @pl.loop(0, steps)
    def _(step):
        mixed, taps_grad = [], []
        for which in range(4):
            s = step * 4 + which
            conv = mix_ref[block_rows(s), :].astype(bf16).astype(f32)
            mix_ref[block_rows(s), :] = conv
            mixed.append(feat_ref[0, s] * conv)
            taps_grad.append(swap_pieces(gate_ref[back_block(s), :]))
        put(step, 0, mixed)
        put(step, 4, taps_grad)

    all_sums = []
    for index in range(3):

        def backward(count, carry, index=index):
            step = steps - 1 - count
            kept, sums = carry
            grads = [None] * 4
            for which in (3, 2, 1, 0):
                s = step * 4 + which
                if index == 0:
                    grad = raw_ref[3, s] * mix_ref[block_rows(s), :]
                else:
                    grad = res_ref[back_block(s), :] * feat_ref[3 - index, s]
                raw = raw_ref[index, s]
                rolled = tuple(pltpu.roll(grad, LANES - j, 1) for j in range(1, TAPS))
                total = w_ref[index * TAPS] * grad
                new_sums = [sums[0] + raw * grad]
                for j in range(1, TAPS):
                    shifted = jnp.where(lane < LANES - j, rolled[j - 1], kept[j - 1])
                    total = total + w_ref[index * TAPS + j] * shifted
                    new_sums.append(sums[j] + raw * shifted)
                kept, sums = rolled, tuple(new_sums)
                grads[which] = total
            put(step, index + 1, grads)
            return kept, sums

        _, sums = lax.fori_loop(0, steps, backward, ((zero,) * (TAPS - 1), (zero,) * TAPS))
        all_sums += sums

    high = zero
    low = zero
    for index, value in enumerate(all_sums):
        total = jnp.sum(value, axis=1, keepdims=True) * scale
        coarse = total.astype(bf16).astype(f32)
        high = jnp.where(lane == index, coarse, high)
        low = jnp.where(lane == index + 32, total - coarse, low)
    both = [high + low] * 4

    @pl.loop(0, steps)
    def _(step):
        put(step, 5, both)


def on_device(query_raw, key_raw, value_raw, featurizer, filter_taps, cotangent):
    tok_rows, channels = query_raw.shape
    blocks = lax.axis_size(SEQ)
    devices = lax.axis_size(SEQ_CH)
    small = pltpu.CompilerParams(vmem_limit_bytes=12 * MIB)
    large = pltpu.CompilerParams(vmem_limit_bytes=20 * MIB)
    sent = jax.ShapeDtypeStruct((devices, 2, WIDTH), bf16)
    sources = (query_raw, key_raw, value_raw, cotangent, filter_taps, featurizer)

    packed = pl.pallas_call(
        pack_kernel,
        in_specs=[pl.BlockSpec(memory_space=pltpu.MemorySpace.HBM)] * len(sources),
        out_shape=sent,
        scratch_shapes=[pltpu.VMEM(source.shape, source.dtype) for source in sources]
        + [pltpu.VMEM((LANES, channels), f32), pltpu.SemaphoreType.DMA((len(sources),))],
        compiler_params=pltpu.CompilerParams(vmem_limit_bytes=60 * MIB),
        name="pack",
    )(*sources)
    received = lax.all_to_all(packed, SEQ_CH, split_axis=0, concat_axis=0, tiled=True)

    flat = pltpu.VMEM((blocks * OWN, LANES), f32)
    by_channel = pltpu.VMEM((OWN, 2 * blocks, LANES), f32)
    outgoing = pl.pallas_call(
        functools.partial(owner_kernel, blocks=blocks, scale=(blocks * LANES) ** -0.5),
        out_shape=sent,
        scratch_shapes=[
            pltpu.VMEM((3 * TAPS, OWN, LANES), f32),
            pltpu.VMEM((4, blocks, OWN, LANES), f32),
            pltpu.VMEM((3, blocks, OWN, LANES), f32),
            flat,
            flat,
            flat,
            by_channel,
            by_channel,
            by_channel,
            flat,
        ],
        compiler_params=large,
        name="owner",
    )(received)
    returned = lax.all_to_all(outgoing, SEQ_CH, split_axis=0, concat_axis=0, tiled=True)

    here = jax.ShapeDtypeStruct((tok_rows, channels), bf16)
    return pl.pallas_call(
        unpack_kernel,
        out_shape=(here,) * 4
        + (
            jax.ShapeDtypeStruct(filter_taps.shape, f32),
            jax.ShapeDtypeStruct(featurizer.shape, f32),
        ),
        compiler_params=small,
        name="unpack",
    )(returned)


def solution(mesh):
    finer = Mesh(mesh.devices.reshape(2, 8, 4, mesh.shape["ch"]), ("seq_0", "seq_1", "seq_2", "ch"))
    placed = (
        P(SEQ, "ch"),
        P(SEQ, "ch"),
        P(SEQ, "ch"),
        P(None, None, "ch"),
        P(SEQ_CH, None),
        P(SEQ, "ch"),
    )
    return jax.shard_map(
        on_device,
        mesh=finer,
        in_specs=placed,
        out_specs=(
            P(SEQ, "ch"),
            P(SEQ, "ch"),
            P(SEQ, "ch"),
            P(SEQ, "ch"),
            P(SEQ_CH, None),
            P(None, None, "ch"),
        ),
        check_vma=False,
    )
```

```python
import functools

import jax
import jax.numpy as jnp
from jax import lax
from jax.experimental import pallas as pl
from jax.experimental.pallas import tpu as pltpu
from jax.sharding import Mesh
from jax.sharding import PartitionSpec as P

TAPS = 7
SEQ = ("seq_0", "seq_1", "seq_2")
SEQ_CH = ("seq_0", "seq_1", "seq_2", "ch")
LANES = 128
OWN = 8
GROUPS = 4
PIECE = LANES // GROUPS
DEPTH = 12
WIDTH = 6 * LANES
MIB = 1024 * 1024

f32 = jnp.float32
bf16 = jnp.bfloat16


def pack_kernel(*refs):
    sources, out_ref, copies = refs[:6], refs[6], refs[7:13]
    weight_ref, sems = refs[13:]
    moves = [
        pltpu.make_async_copy(source, copy, sems.at[index])
        for index, (source, copy) in enumerate(zip(sources, copies))
    ]
    for move in moves:
        move.start()
    pairs = (out_ref.shape[0], 2, LANES)
    wide = out_ref.shape[0] * 2

    def put(index, rows):
        out_ref[:, :, index * LANES : (index + 1) * LANES] = rows.T.astype(bf16).reshape(pairs)

    weight_ref[...] = jnp.zeros_like(weight_ref)
    for index in range(4):
        moves[index].wait()
        put(index, copies[index][...].astype(f32))
    moves[4].wait()
    taps = copies[4][...].astype(f32)
    put(4, jnp.concatenate([taps[:, g * wide : (g + 1) * wide] for g in range(GROUPS)], axis=0))
    moves[5].wait()
    for index in range(3):
        weight = copies[5][index]
        coarse = weight.astype(bf16).astype(f32)
        row = TAPS * index
        weight_ref[row : row + TAPS, :] = coarse
        weight_ref[row + 32 : row + 32 + TAPS, :] = weight - coarse
    put(5, weight_ref[...])


def unpack_kernel(in_ref, mixed_ref, qg_ref, kg_ref, vg_ref, fg_ref, wg_ref):
    wide = in_ref.shape[0] * 2

    def turned(index):
        rows = in_ref[:, :, index * LANES : (index + 1) * LANES].reshape(wide, LANES)
        return rows.astype(f32).T

    for index, ref in enumerate((mixed_ref, qg_ref, kg_ref, vg_ref)):
        ref[...] = turned(index).astype(bf16)
    taps_grad = turned(4)
    for g in range(GROUPS):
        fg_ref[:, g * wide : (g + 1) * wide] = taps_grad[g * PIECE : (g + 1) * PIECE]
    sums = turned(5)
    total = sums[0:24] + sums[32:56]
    for index in range(3):
        wg_ref[index] = total[TAPS * index : TAPS * (index + 1)]


def owner_kernel(
    in_ref,
    out_ref,
    w_ref,
    raw_ref,
    feat_ref,
    mix_ref,
    gate_ref,
    tap_ref,
    xm_ref,
    xh_ref,
    res_ref,
    left_ref,
    lhs_ref,
    acc_ref,
    *,
    blocks,
    scale,
):
    lane = lax.broadcasted_iota(jnp.int32, (OWN, LANES), 1)
    row = lax.broadcasted_iota(jnp.int32, (OWN, LANES), 0)
    group = row // 2
    piece = lane // PIECE
    flip_row = lax.broadcasted_iota(jnp.int32, (LANES, LANES), 0)
    flip_col = lax.broadcasted_iota(jnp.int32, (LANES, LANES), 1)
    flip = (flip_row + flip_col == LANES - 1).astype(f32).astype(bf16)
    zero = jnp.zeros((OWN, LANES), f32)
    steps = blocks // 4

    def swap_pieces(value):
        result = value
        for k in range(1, GROUPS):
            moved = pltpu.roll(pltpu.roll(value, PIECE * k, 1), OWN - 2 * k, 0)
            result = jnp.where(piece == (group + k) % GROUPS, moved, result)
        return result

    def summed(terms):
        while len(terms) > 1:
            pairs = [one + two for one, two in zip(terms[::2], terms[1::2])]
            terms = pairs + terms[len(pairs) * 2 :]
        return terms[0]

    def block_rows(s):
        return pl.ds(pl.multiple_of(s * OWN, OWN), OWN)

    def taken(step, index):
        rows = in_ref[pl.ds(step * 16, 16), :, index * LANES : (index + 1) * LANES]
        return rows.reshape(4 * OWN, LANES).astype(f32)

    weights = taken(0, 5)[:OWN]
    weights = weights + pltpu.roll(weights, LANES - 32, 1)
    for index in range(3 * TAPS):
        w_ref[index] = jnp.broadcast_to(weights[:, index : index + 1], (OWN, LANES))

    @pl.loop(0, steps, unroll=16)
    def _(step):
        for index in range(5):
            values = taken(step, index)
            for which in range(4):
                s = step * 4 + which
                value = values[which * OWN : (which + 1) * OWN]
                if index < 4:
                    raw_ref[index, s] = value
                else:
                    tap_ref[block_rows(s), :] = swap_pieces(value)

    for index in range(3):

        def forward(step, kept, index=index):
            for which in range(64):
                s = step * 64 + which
                block = raw_ref[index, s]
                rolled = tuple(pltpu.roll(block, j, 1) for j in range(1, TAPS))
                terms = [w_ref[index * TAPS] * block]
                for j in range(1, TAPS):
                    shifted = jnp.where(lane >= j, rolled[j - 1], kept[j - 1])
                    terms.append(w_ref[index * TAPS + j] * shifted)
                total = summed(terms)
                kept = rolled
                feat_ref[index, s] = total
                if index == 0:
                    gate_ref[block_rows(s), :] = (raw_ref[3, s] * total).astype(bf16).astype(f32)
                if index == 2:
                    mix_ref[block_rows(s), :] = (feat_ref[1, s] * total).astype(bf16).astype(f32)
            return kept

        lax.fori_loop(0, blocks // 64, forward, (zero,) * (TAPS - 1))

    res_ref[...] = jnp.dot(gate_ref[...].astype(bf16), flip, preferred_element_type=f32)

    for b in range(GROUPS):
        for o in range(2):
            left_ref[o, b, : DEPTH * OWN, :] = jnp.zeros((DEPTH * OWN, LANES), f32)

    def lay(step, carry):
        carry = list(carry)
        for which in range(4):
            s = step * 4 + which
            sources = (mix_ref[block_rows(s), :], res_ref[block_rows(blocks - 1 - s), :])
            rows = pl.ds(pl.multiple_of((s + DEPTH) * OWN, OWN), OWN)
            for o, value in enumerate(sources):
                turns = (value,) + tuple(pltpu.roll(value, PIECE * k, 1) for k in range(1, GROUPS))
                history = (turns,) + carry[o]
                for b in range(GROUPS):
                    laid = history[0][-b % GROUPS]
                    for p in range(1, GROUPS):
                        laid = jnp.where(piece == p, history[p][(p - b) % GROUPS], laid)
                    left_ref[o, b, rows, :] = laid
                carry[o] = history[: GROUPS - 1]
        return tuple(carry)

    blank = ((zero,) * GROUPS,) * (GROUPS - 1)
    lax.fori_loop(0, steps, lay, (blank, blank), unroll=16)

    for r in range(OWN):
        for source, target in ((mix_ref, xm_ref), (tap_ref, xh_ref)):
            target[r] = source[pl.ds(r, blocks, stride=OWN), :]

    tile_row = lax.broadcasted_iota(jnp.int32, (PIECE, LANES), 0)
    tile_col = lax.broadcasted_iota(jnp.int32, (PIECE, LANES), 1)
    causal = tile_col >= tile_row
    full_row = lax.broadcasted_iota(jnp.int32, (blocks, LANES), 0)
    full_col = lax.broadcasted_iota(jnp.int32, (blocks, LANES), 1)
    reach = 4 * GROUPS

    def long_conv(r, signal_ref, operands):
        before = jnp.zeros((PIECE, LANES), f32)
        for part in range(blocks // reach):
            tiles = []
            for mu in range(part * reach, (part + 1) * reach):
                line = jnp.broadcast_to(signal_ref[r, mu : mu + 1, :], (PIECE, LANES))
                turned = pltpu.roll(line, 0, 1, stride=1, stride_axis=0)
                tiles.append(jnp.where(causal, turned, before).astype(bf16))
                before = turned
            right = jnp.concatenate(tiles, axis=0)
            start = part * reach
            height = blocks - start
            for o in operands:
                left = lhs_ref[o, :, :height, :].reshape(GROUPS * height, reach * PIECE)
                product = jnp.dot(left, right, preferred_element_type=f32)
                product = product.reshape(GROUPS, height, LANES)
                if part == 0:
                    acc_ref[o] = product
                else:
                    acc_ref[o, :, start:, :] += product

    def gathered(o):
        total = acc_ref[o, 0]
        wrapped = jnp.zeros((blocks, LANES), f32)
        for b in range(1, GROUPS):
            moved = pltpu.roll(acc_ref[o, b], PIECE * b, 1)
            inside = full_col >= PIECE * b
            total = total + jnp.where(inside, moved, 0.0)
            wrapped = wrapped + jnp.where(inside, 0.0, moved)
        return total + jnp.where(full_row > 0, pltpu.roll(wrapped, 1, 0), 0.0)

    @pl.loop(0, OWN, unroll=4)
    def _(r):
        for o in range(2):
            for b in range(GROUPS):
                for depth in range(GROUPS):
                    rows = pl.ds((DEPTH - GROUPS * depth) * OWN + r, blocks, stride=OWN)
                    lanes = slice(depth * LANES, (depth + 1) * LANES)
                    lhs_ref[o, b, :, lanes] = left_ref[o, b, rows, :].astype(bf16)
        here = pl.ds(r, blocks, stride=OWN)
        long_conv(r, xm_ref, (1,))
        tap_ref[here, :] = gathered(1) * scale
        long_conv(r, xh_ref, (0, 1))
        mix_ref[here, :] = gathered(0)
        gate_ref[here, :] = gathered(1)

    res_ref[...] = jnp.dot(gate_ref[...].astype(bf16), flip, preferred_element_type=f32)
    gate_ref[...] = jnp.dot(tap_ref[...].astype(bf16), flip, preferred_element_type=f32)

    def put(step, index, values):
        rows = jnp.concatenate(values, axis=0).astype(bf16).reshape(16, 2, LANES)
        out_ref[pl.ds(step * 16, 16), :, index * LANES : (index + 1) * LANES] = rows

    def back_block(s):
        return block_rows(blocks - 1 - s)

    @pl.loop(0, steps, unroll=16)
    def _(step):
        mixed, taps_grad = [], []
        for which in range(4):
            s = step * 4 + which
            conv = mix_ref[block_rows(s), :].astype(bf16).astype(f32)
            mix_ref[block_rows(s), :] = conv
            mixed.append(feat_ref[0, s] * conv)
            taps_grad.append(swap_pieces(gate_ref[back_block(s), :]))
        put(step, 0, mixed)
        put(step, 4, taps_grad)

    all_sums = []
    for index in range(3):

        def backward(count, carry, index=index):
            kept, sums = carry
            for sub in reversed(range(64 // 4)):
                step = (blocks // 64 - 1 - count) * (64 // 4) + sub
                grads = [None] * 4
                for which in (3, 2, 1, 0):
                    s = step * 4 + which
                    if index == 0:
                        grad = raw_ref[3, s] * mix_ref[block_rows(s), :]
                    else:
                        grad = res_ref[back_block(s), :] * feat_ref[3 - index, s]
                    raw = raw_ref[index, s]
                    rolled = tuple(pltpu.roll(grad, LANES - j, 1) for j in range(1, TAPS))
                    terms = [w_ref[index * TAPS] * grad]
                    new_sums = [sums[0] + raw * grad]
                    for j in range(1, TAPS):
                        shifted = jnp.where(lane < LANES - j, rolled[j - 1], kept[j - 1])
                        terms.append(w_ref[index * TAPS + j] * shifted)
                        new_sums.append(sums[j] + raw * shifted)
                    kept, sums = rolled, tuple(new_sums)
                    grads[which] = summed(terms)
                put(step, index + 1, grads)
            return kept, sums

        _, sums = lax.fori_loop(
            0, blocks // 64, backward, ((zero,) * (TAPS - 1), (zero,) * TAPS)
        )
        all_sums += sums

    high = zero
    low = zero
    for index, value in enumerate(all_sums):
        total = jnp.sum(value, axis=1, keepdims=True) * scale
        coarse = total.astype(bf16).astype(f32)
        high = jnp.where(lane == index, coarse, high)
        low = jnp.where(lane == index + 32, total - coarse, low)
    both = [high + low] * 4

    for step in range(steps):
        put(step, 5, both)


def on_device(query_raw, key_raw, value_raw, featurizer, filter_taps, cotangent):
    tok_rows, channels = query_raw.shape
    blocks = lax.axis_size(SEQ)
    devices = lax.axis_size(SEQ_CH)
    small = pltpu.CompilerParams(vmem_limit_bytes=12 * MIB)
    large = pltpu.CompilerParams(vmem_limit_bytes=20 * MIB)
    sent = jax.ShapeDtypeStruct((devices, 2, WIDTH), bf16)
    sources = (query_raw, key_raw, value_raw, cotangent, filter_taps, featurizer)

    packed = pl.pallas_call(
        pack_kernel,
        in_specs=[pl.BlockSpec(memory_space=pltpu.MemorySpace.HBM)] * len(sources),
        out_shape=sent,
        scratch_shapes=[pltpu.VMEM(source.shape, source.dtype) for source in sources]
        + [pltpu.VMEM((LANES, channels), f32), pltpu.SemaphoreType.DMA((len(sources),))],
        compiler_params=pltpu.CompilerParams(vmem_limit_bytes=60 * MIB),
        name="pack",
    )(*sources)
    received = lax.all_to_all(packed, SEQ_CH, split_axis=0, concat_axis=0, tiled=True)

    flat = pltpu.VMEM((blocks * OWN, LANES), f32)
    by_channel = pltpu.VMEM((OWN, blocks, LANES), f32)
    outgoing = pl.pallas_call(
        functools.partial(owner_kernel, blocks=blocks, scale=(blocks * LANES) ** -0.5),
        out_shape=sent,
        scratch_shapes=[
            pltpu.VMEM((3 * TAPS, OWN, LANES), f32),
            pltpu.VMEM((4, blocks, OWN, LANES), f32),
            pltpu.VMEM((3, blocks, OWN, LANES), f32),
            flat,
            flat,
            flat,
            by_channel,
            by_channel,
            flat,
            pltpu.VMEM((2, GROUPS, (blocks + DEPTH) * OWN, LANES), f32),
            pltpu.VMEM((2, GROUPS, blocks, GROUPS * LANES), bf16),
            pltpu.VMEM((2, GROUPS, blocks, LANES), f32),
        ],
        compiler_params=large,
        name="owner",
    )(received)
    returned = lax.all_to_all(outgoing, SEQ_CH, split_axis=0, concat_axis=0, tiled=True)

    here = jax.ShapeDtypeStruct((tok_rows, channels), bf16)
    return pl.pallas_call(
        unpack_kernel,
        out_shape=(here,) * 4
        + (
            jax.ShapeDtypeStruct(filter_taps.shape, f32),
            jax.ShapeDtypeStruct(featurizer.shape, f32),
        ),
        compiler_params=small,
        name="unpack",
    )(returned)


def solution(mesh):
    finer = Mesh(mesh.devices.reshape(2, 8, 4, mesh.shape["ch"]), ("seq_0", "seq_1", "seq_2", "ch"))
    placed = (
        P(SEQ, "ch"),
        P(SEQ, "ch"),
        P(SEQ, "ch"),
        P(None, None, "ch"),
        P(SEQ_CH, None),
        P(SEQ, "ch"),
    )
    return jax.shard_map(
        on_device,
        mesh=finer,
        in_specs=placed,
        out_specs=(
            P(SEQ, "ch"),
            P(SEQ, "ch"),
            P(SEQ, "ch"),
            P(SEQ, "ch"),
            P(SEQ_CH, None),
            P(None, None, "ch"),
        ),
        check_vma=False,
    )
```

```python
import functools

import jax
import jax.numpy as jnp
from jax import lax
from jax.experimental import pallas as pl
from jax.experimental.pallas import tpu as pltpu
from jax.sharding import Mesh
from jax.sharding import PartitionSpec as P

TAPS = 7
SEQ = ("seq_0", "seq_1", "seq_2")
SEQ_CH = ("seq_0", "seq_1", "seq_2", "ch")
LANES = 128
OWN = 8
GROUPS = 4
PIECE = LANES // GROUPS
DEPTH = 12
MIB = 1024 * 1024

f32 = jnp.float32
bf16 = jnp.bfloat16


def pack_kernel(*refs):
    sources, out_ref, copies, sems = refs[:5], refs[5], refs[6:11], refs[11]
    moves = [
        pltpu.make_async_copy(source, copy, sems.at[index])
        for index, (source, copy) in enumerate(zip(sources, copies))
    ]
    for move in moves:
        move.start()
    pairs = (out_ref.shape[0], 2, LANES)
    wide = out_ref.shape[0] * 2

    def put(index, rows):
        out_ref[:, :, index * LANES : (index + 1) * LANES] = rows.T.astype(bf16).reshape(pairs)

    for index in range(4):
        moves[index].wait()
        put(index, copies[index][...].astype(f32))
    moves[4].wait()
    taps = copies[4][...].astype(f32)
    put(4, jnp.concatenate([taps[:, g * wide : (g + 1) * wide] for g in range(GROUPS)], axis=0))


def unpack_kernel(in_ref, mixed_ref, qg_ref, kg_ref, vg_ref, fg_ref, wg_ref):
    wide = in_ref.shape[0] * 2

    def turned(index):
        rows = in_ref[:, :, index * LANES : (index + 1) * LANES].reshape(wide, LANES)
        return rows.astype(f32).T

    for index, ref in enumerate((mixed_ref, qg_ref, kg_ref, vg_ref)):
        ref[...] = turned(index).astype(bf16)
    taps_grad = turned(4)
    for g in range(GROUPS):
        fg_ref[:, g * wide : (g + 1) * wide] = taps_grad[g * PIECE : (g + 1) * PIECE]
    sums = turned(5)
    total = sums[0:24] + sums[32:56]
    for index in range(3):
        wg_ref[index] = total[TAPS * index : TAPS * (index + 1)]


def owner_kernel(
    in_ref,
    own_ref,
    out_ref,
    w_ref,
    raw_ref,
    feat_ref,
    mix_ref,
    gate_ref,
    tap_ref,
    xm_ref,
    xh_ref,
    res_ref,
    left_ref,
    lhs_ref,
    acc_ref,
    *,
    blocks,
    scale,
):
    lane = lax.broadcasted_iota(jnp.int32, (OWN, LANES), 1)
    row = lax.broadcasted_iota(jnp.int32, (OWN, LANES), 0)
    group = row // 2
    piece = lane // PIECE
    flip_row = lax.broadcasted_iota(jnp.int32, (LANES, LANES), 0)
    flip_col = lax.broadcasted_iota(jnp.int32, (LANES, LANES), 1)
    flip = (flip_row + flip_col == LANES - 1).astype(f32).astype(bf16)
    zero = jnp.zeros((OWN, LANES), f32)
    steps = blocks // 4

    def swap_pieces(value):
        result = value
        for k in range(1, GROUPS):
            moved = pltpu.roll(pltpu.roll(value, PIECE * k, 1), OWN - 2 * k, 0)
            result = jnp.where(piece == (group + k) % GROUPS, moved, result)
        return result

    def summed(terms):
        while len(terms) > 1:
            pairs = [one + two for one, two in zip(terms[::2], terms[1::2])]
            terms = pairs + terms[len(pairs) * 2 :]
        return terms[0]

    def block_rows(s):
        return pl.ds(pl.multiple_of(s * OWN, OWN), OWN)

    def taken(step, index):
        rows = in_ref[pl.ds(step * 16, 16), :, index * LANES : (index + 1) * LANES]
        return rows.reshape(4 * OWN, LANES).astype(f32)

    for index in range(3 * TAPS):
        w_ref[index] = jnp.broadcast_to(own_ref[:, index : index + 1], (OWN, LANES))

    @pl.loop(0, steps, unroll=16)
    def _(step):
        for index in range(5):
            values = taken(step, index)
            for which in range(4):
                s = step * 4 + which
                value = values[which * OWN : (which + 1) * OWN]
                if index < 4:
                    raw_ref[index, s] = value
                else:
                    tap_ref[block_rows(s), :] = swap_pieces(value)

    for index in range(3):

        def forward(step, kept, index=index):
            for which in range(64):
                s = step * 64 + which
                block = raw_ref[index, s]
                rolled = tuple(pltpu.roll(block, j, 1) for j in range(1, TAPS))
                terms = [w_ref[index * TAPS] * block]
                for j in range(1, TAPS):
                    shifted = jnp.where(lane >= j, rolled[j - 1], kept[j - 1])
                    terms.append(w_ref[index * TAPS + j] * shifted)
                total = summed(terms)
                kept = rolled
                feat_ref[index, s] = total
                if index == 0:
                    gate_ref[block_rows(s), :] = (raw_ref[3, s] * total).astype(bf16).astype(f32)
                if index == 2:
                    mix_ref[block_rows(s), :] = (feat_ref[1, s] * total).astype(bf16).astype(f32)
            return kept

        lax.fori_loop(0, blocks // 64, forward, (zero,) * (TAPS - 1))

    res_ref[...] = jnp.dot(gate_ref[...].astype(bf16), flip, preferred_element_type=f32)

    for b in range(GROUPS):
        for o in range(2):
            left_ref[o, b, : DEPTH * OWN, :] = jnp.zeros((DEPTH * OWN, LANES), f32)

    def lay(step, carry):
        carry = list(carry)
        for which in range(4):
            s = step * 4 + which
            sources = (mix_ref[block_rows(s), :], res_ref[block_rows(blocks - 1 - s), :])
            rows = pl.ds(pl.multiple_of((s + DEPTH) * OWN, OWN), OWN)
            for o, value in enumerate(sources):
                turns = (value,) + tuple(pltpu.roll(value, PIECE * k, 1) for k in range(1, GROUPS))
                history = (turns,) + carry[o]
                for b in range(GROUPS):
                    laid = history[0][-b % GROUPS]
                    for p in range(1, GROUPS):
                        laid = jnp.where(piece == p, history[p][(p - b) % GROUPS], laid)
                    left_ref[o, b, rows, :] = laid
                carry[o] = history[: GROUPS - 1]
        return tuple(carry)

    blank = ((zero,) * GROUPS,) * (GROUPS - 1)
    lax.fori_loop(0, steps, lay, (blank, blank), unroll=16)

    for r in range(OWN):
        for source, target in ((mix_ref, xm_ref), (tap_ref, xh_ref)):
            target[r] = source[pl.ds(r, blocks, stride=OWN), :]

    tile_row = lax.broadcasted_iota(jnp.int32, (PIECE, LANES), 0)
    tile_col = lax.broadcasted_iota(jnp.int32, (PIECE, LANES), 1)
    causal = tile_col >= tile_row
    full_row = lax.broadcasted_iota(jnp.int32, (blocks, LANES), 0)
    full_col = lax.broadcasted_iota(jnp.int32, (blocks, LANES), 1)
    reach = 4 * GROUPS

    def toeplitz(r, signal_ref, part, before):
        tiles = []
        for mu in range(part * reach, (part + 1) * reach):
            line = jnp.broadcast_to(signal_ref[r, mu : mu + 1, :], (PIECE, LANES))
            turned = pltpu.roll(line, 0, 1, stride=1, stride_axis=0)
            tiles.append(jnp.where(causal, turned, before).astype(bf16))
            before = turned
        return jnp.concatenate(tiles, axis=0), before

    def long_convs(r):
        before_taps = before_mix = jnp.zeros((PIECE, LANES), f32)
        for part in range(blocks // reach):
            taps, before_taps = toeplitz(r, xh_ref, part, before_taps)
            mix, before_mix = toeplitz(r, xm_ref, part, before_mix)
            start = part * reach
            height = blocks - start
            flat = (GROUPS * height, reach * PIECE)
            one = jnp.dot(lhs_ref[0, :, :height, :].reshape(flat), taps, preferred_element_type=f32)
            two = jnp.dot(
                lhs_ref[1, :, :height, :].reshape(flat),
                jnp.concatenate([taps, mix], axis=1),
                preferred_element_type=f32,
            )
            for o, product in enumerate((one, two[:, :LANES], two[:, LANES:])):
                product = product.reshape(GROUPS, height, LANES)
                if part == 0:
                    acc_ref[o] = product
                else:
                    acc_ref[o, :, start:, :] += product

    def gathered(o):
        total = acc_ref[o, 0]
        wrapped = jnp.zeros((blocks, LANES), f32)
        for b in range(1, GROUPS):
            moved = pltpu.roll(acc_ref[o, b], PIECE * b, 1)
            inside = full_col >= PIECE * b
            total = total + jnp.where(inside, moved, 0.0)
            wrapped = wrapped + jnp.where(inside, 0.0, moved)
        return total + jnp.where(full_row > 0, pltpu.roll(wrapped, 1, 0), 0.0)

    @pl.loop(0, OWN, unroll=4)
    def _(r):
        for o in range(2):
            for b in range(GROUPS):
                for depth in range(GROUPS):
                    rows = pl.ds((DEPTH - GROUPS * depth) * OWN + r, blocks, stride=OWN)
                    lanes = slice(depth * LANES, (depth + 1) * LANES)
                    lhs_ref[o, b, :, lanes] = left_ref[o, b, rows, :].astype(bf16)
        here = pl.ds(r, blocks, stride=OWN)
        long_convs(r)
        mix_ref[here, :] = gathered(0)
        gate_ref[here, :] = gathered(1)
        tap_ref[here, :] = gathered(2) * scale

    res_ref[...] = jnp.dot(gate_ref[...].astype(bf16), flip, preferred_element_type=f32)
    gate_ref[...] = jnp.dot(tap_ref[...].astype(bf16), flip, preferred_element_type=f32)

    def put(step, index, values):
        rows = jnp.concatenate(values, axis=0).astype(bf16).reshape(16, 2, LANES)
        out_ref[pl.ds(step * 16, 16), :, index * LANES : (index + 1) * LANES] = rows

    def back_block(s):
        return block_rows(blocks - 1 - s)

    @pl.loop(0, steps, unroll=16)
    def _(step):
        mixed, taps_grad = [], []
        for which in range(4):
            s = step * 4 + which
            conv = mix_ref[block_rows(s), :].astype(bf16).astype(f32)
            mix_ref[block_rows(s), :] = conv
            mixed.append(feat_ref[0, s] * conv)
            taps_grad.append(swap_pieces(gate_ref[back_block(s), :]))
        put(step, 0, mixed)
        put(step, 4, taps_grad)

    all_sums = []
    for index in range(3):

        def backward(count, carry, index=index):
            kept, sums = carry
            for sub in reversed(range(64 // 4)):
                step = (blocks // 64 - 1 - count) * (64 // 4) + sub
                grads = [None] * 4
                for which in (3, 2, 1, 0):
                    s = step * 4 + which
                    if index == 0:
                        grad = raw_ref[3, s] * mix_ref[block_rows(s), :]
                    else:
                        grad = res_ref[back_block(s), :] * feat_ref[3 - index, s]
                    raw = raw_ref[index, s]
                    rolled = tuple(pltpu.roll(grad, LANES - j, 1) for j in range(1, TAPS))
                    terms = [w_ref[index * TAPS] * grad]
                    new_sums = [sums[0] + raw * grad]
                    for j in range(1, TAPS):
                        shifted = jnp.where(lane < LANES - j, rolled[j - 1], kept[j - 1])
                        terms.append(w_ref[index * TAPS + j] * shifted)
                        new_sums.append(sums[j] + raw * shifted)
                    kept, sums = rolled, tuple(new_sums)
                    grads[which] = summed(terms)
                put(step, index + 1, grads)
            return kept, sums

        _, sums = lax.fori_loop(
            0, blocks // 64, backward, ((zero,) * (TAPS - 1), (zero,) * TAPS)
        )
        all_sums += sums

    high = zero
    low = zero
    for index, value in enumerate(all_sums):
        total = jnp.sum(value, axis=1, keepdims=True) * scale
        coarse = total.astype(bf16).astype(f32)
        high = jnp.where(lane == index, coarse, high)
        low = jnp.where(lane == index + 32, total - coarse, low)
    both = [high + low] * 4

    for step in range(steps):
        put(step, 5, both)


def on_device(query_raw, key_raw, value_raw, featurizer, filter_taps, cotangent):
    tok_rows, channels = query_raw.shape
    blocks = lax.axis_size(SEQ)
    devices = lax.axis_size(SEQ_CH)
    small = pltpu.CompilerParams(vmem_limit_bytes=12 * MIB)
    large = pltpu.CompilerParams(vmem_limit_bytes=20 * MIB)
    me = lax.axis_index(SEQ_CH)
    sources = (query_raw, key_raw, value_raw, cotangent, filter_taps)

    packed = pl.pallas_call(
        pack_kernel,
        in_specs=[pl.BlockSpec(memory_space=pltpu.MemorySpace.HBM)] * len(sources),
        out_shape=jax.ShapeDtypeStruct((devices, 2, 5 * LANES), bf16),
        scratch_shapes=[pltpu.VMEM(source.shape, source.dtype) for source in sources]
        + [pltpu.SemaphoreType.DMA((len(sources),))],
        compiler_params=pltpu.CompilerParams(vmem_limit_bytes=60 * MIB),
        name="pack",
    )(*sources)
    received = lax.all_to_all(packed, SEQ_CH, split_axis=0, concat_axis=0, tiled=True)

    weights = lax.all_gather(featurizer, "ch")
    weights = lax.dynamic_slice(weights, (0, 0, 0, 2 * me), (GROUPS, 3, TAPS, 2))
    weights = weights.transpose(0, 3, 1, 2).reshape(OWN, 3 * TAPS)

    flat = pltpu.VMEM((blocks * OWN, LANES), f32)
    by_channel = pltpu.VMEM((OWN, blocks, LANES), f32)
    outgoing = pl.pallas_call(
        functools.partial(owner_kernel, blocks=blocks, scale=(blocks * LANES) ** -0.5),
        out_shape=jax.ShapeDtypeStruct((devices, 2, 6 * LANES), bf16),
        scratch_shapes=[
            pltpu.VMEM((3 * TAPS, OWN, LANES), f32),
            pltpu.VMEM((4, blocks, OWN, LANES), f32),
            pltpu.VMEM((3, blocks, OWN, LANES), f32),
            flat,
            flat,
            flat,
            by_channel,
            by_channel,
            flat,
            pltpu.VMEM((2, GROUPS, (blocks + DEPTH) * OWN, LANES), f32),
            pltpu.VMEM((2, GROUPS, blocks, GROUPS * LANES), bf16),
            pltpu.VMEM((3, GROUPS, blocks, LANES), f32),
        ],
        compiler_params=large,
        name="owner",
    )(received, weights)
    returned = lax.all_to_all(outgoing, SEQ_CH, split_axis=0, concat_axis=0, tiled=True)

    here = jax.ShapeDtypeStruct((tok_rows, channels), bf16)
    return pl.pallas_call(
        unpack_kernel,
        out_shape=(here,) * 4
        + (
            jax.ShapeDtypeStruct(filter_taps.shape, f32),
            jax.ShapeDtypeStruct(featurizer.shape, f32),
        ),
        compiler_params=small,
        name="unpack",
    )(returned)


def solution(mesh):
    finer = Mesh(mesh.devices.reshape(2, 8, 4, mesh.shape["ch"]), ("seq_0", "seq_1", "seq_2", "ch"))
    placed = (
        P(SEQ, "ch"),
        P(SEQ, "ch"),
        P(SEQ, "ch"),
        P(None, None, "ch"),
        P(SEQ_CH, None),
        P(SEQ, "ch"),
    )
    return jax.shard_map(
        on_device,
        mesh=finer,
        in_specs=placed,
        out_specs=(
            P(SEQ, "ch"),
            P(SEQ, "ch"),
            P(SEQ, "ch"),
            P(SEQ, "ch"),
            P(SEQ_CH, None),
            P(None, None, "ch"),
        ),
        check_vma=False,
    )
```

```python
import functools

import jax
import jax.numpy as jnp
from jax import lax
from jax.experimental import pallas as pl
from jax.experimental.pallas import tpu as pltpu
from jax.sharding import Mesh
from jax.sharding import PartitionSpec as P

TAPS = 7
SEQ = ("seq_0", "seq_1", "seq_2")
SEQ_CH = ("seq_0", "seq_1", "seq_2", "ch")
LANES = 128
OWN = 8
GROUPS = 4
PIECE = LANES // GROUPS
DEPTH = 12
MIB = 1024 * 1024

f32 = jnp.float32
bf16 = jnp.bfloat16


def pack_kernel(*refs):
    sources, out_ref, copies, sems = refs[:5], refs[5], refs[6:11], refs[11]
    moves = [
        pltpu.make_async_copy(source, copy, sems.at[index])
        for index, (source, copy) in enumerate(zip(sources, copies))
    ]
    for move in moves:
        move.start()
    pairs = (out_ref.shape[0], 2, LANES)
    wide = out_ref.shape[0] * 2

    def put(index, rows):
        out_ref[:, :, index * LANES : (index + 1) * LANES] = rows.T.astype(bf16).reshape(pairs)

    for index in range(4):
        moves[index].wait()
        put(index, copies[index][...].astype(f32))
    moves[4].wait()
    taps = copies[4][...].astype(f32)
    put(4, jnp.concatenate([taps[:, g * wide : (g + 1) * wide] for g in range(GROUPS)], axis=0))


def feat_kernel(q_ref, k_ref, v_ref, w_ref, fq_ref, fk_ref, fv_ref, padded_ref):
    rows, wide = q_ref.shape
    padded_ref[:OWN, :] = jnp.zeros((OWN, wide), f32)
    for index, (ref, out_ref) in enumerate(((q_ref, fq_ref), (k_ref, fk_ref), (v_ref, fv_ref))):
        padded_ref[OWN:, :] = ref[...].astype(f32)
        for column in range(0, wide, LANES):
            part = slice(column, column + LANES)
            total = w_ref[index, 0:1, part] * padded_ref[OWN:, part]
            for j in range(1, TAPS):
                total = total + w_ref[index, j : j + 1, part] * padded_ref[OWN - j : OWN - j + rows, part]
            out_ref[:, part] = total


def unpack_kernel(
    in_ref,
    fq_ref,
    fk_ref,
    fv_ref,
    c_ref,
    w_ref,
    mixed_ref,
    qg_ref,
    kg_ref,
    vg_ref,
    fg_ref,
    wg_ref,
    conv_ref,
    grad_ref,
    edge_ref,
    first_ref,
    padded_ref,
):
    wide = in_ref.shape[0] * 2
    rows = c_ref.shape[0]

    def turned(index):
        values = in_ref[:, :, index * LANES : (index + 1) * LANES].reshape(wide, LANES)
        return values.astype(f32).T

    conv_ref[...] = turned(0)
    grad_ref[...] = turned(1)
    taps_grad = turned(2)
    for g in range(GROUPS):
        fg_ref[:, g * wide : (g + 1) * wide] = taps_grad[g * PIECE : (g + 1) * PIECE]
    edge_ref[:LANES, :] = turned(3)
    total = edge_ref[0:24, :] + edge_ref[32:56, :]
    for index in range(3):
        wg_ref[index] = total[TAPS * index : TAPS * (index + 1)]

    last = slice(LANES, LANES + OWN)
    after = slice(LANES + OWN, LANES + 2 * OWN)
    edge_ref[after, :] = jnp.zeros((OWN, wide), f32)
    for index, ref in enumerate((fq_ref, fk_ref, fv_ref)):
        edge_ref[last, :] = edge_ref[96 + OWN * index : 96 + OWN * (index + 1), :]
        first = ref[:OWN, :]
        for j in range(1, TAPS):
            start = LANES + OWN - j
            first = first + w_ref[index, j : j + 1, :] * edge_ref[start : start + OWN, :]
        first_ref[index] = first

    def feat(index, part):
        ref = (fq_ref, fk_ref, fv_ref)[index]
        return jnp.concatenate([first_ref[index, :, part], ref[OWN:, part]], axis=0)

    for index, out_ref in enumerate((qg_ref, kg_ref, vg_ref)):
        padded_ref[rows:, :] = edge_ref[64 + OWN * index : 64 + OWN * (index + 1), :]
        for column in range(0, wide, LANES):
            part = slice(column, column + LANES)
            if index == 0:
                conv = conv_ref[:, part]
                mixed_ref[:, part] = (feat(0, part) * conv).astype(bf16)
                grad = c_ref[:, part].astype(f32) * conv
            else:
                grad = grad_ref[:, part] * feat(3 - index, part)
            padded_ref[:rows, part] = grad
            total = w_ref[index, 0:1, part] * grad
            for j in range(1, TAPS):
                total = total + w_ref[index, j : j + 1, part] * padded_ref[j : j + rows, part]
            out_ref[:, part] = total.astype(bf16)


def owner_kernel(
    in_ref,
    own_ref,
    out_ref,
    w_ref,
    raw_ref,
    feat_ref,
    mix_ref,
    gate_ref,
    tap_ref,
    xm_ref,
    xh_ref,
    res_ref,
    left_ref,
    lhs_ref,
    acc_ref,
    *,
    blocks,
    scale,
):
    lane = lax.broadcasted_iota(jnp.int32, (OWN, LANES), 1)
    row = lax.broadcasted_iota(jnp.int32, (OWN, LANES), 0)
    group = row // 2
    piece = lane // PIECE
    flip_row = lax.broadcasted_iota(jnp.int32, (LANES, LANES), 0)
    flip_col = lax.broadcasted_iota(jnp.int32, (LANES, LANES), 1)
    flip = (flip_row + flip_col == LANES - 1).astype(f32).astype(bf16)
    zero = jnp.zeros((OWN, LANES), f32)
    steps = blocks // 4

    def swap_pieces(value):
        result = value
        for k in range(1, GROUPS):
            moved = pltpu.roll(pltpu.roll(value, PIECE * k, 1), OWN - 2 * k, 0)
            result = jnp.where(piece == (group + k) % GROUPS, moved, result)
        return result

    def summed(terms):
        while len(terms) > 1:
            pairs = [one + two for one, two in zip(terms[::2], terms[1::2])]
            terms = pairs + terms[len(pairs) * 2 :]
        return terms[0]

    def block_rows(s):
        return pl.ds(pl.multiple_of(s * OWN, OWN), OWN)

    def taken(step, index):
        rows = in_ref[pl.ds(step * 16, 16), :, index * LANES : (index + 1) * LANES]
        return rows.reshape(4 * OWN, LANES).astype(f32)

    for index in range(3 * TAPS):
        w_ref[index] = jnp.broadcast_to(own_ref[:, index : index + 1], (OWN, LANES))

    @pl.loop(0, steps, unroll=16)
    def _(step):
        for index in range(5):
            values = taken(step, index)
            for which in range(4):
                s = step * 4 + which
                value = values[which * OWN : (which + 1) * OWN]
                if index < 4:
                    raw_ref[index, s] = value
                else:
                    tap_ref[block_rows(s), :] = swap_pieces(value)

    for index in range(3):

        def forward(step, kept, index=index):
            for which in range(64):
                s = step * 64 + which
                block = raw_ref[index, s]
                rolled = tuple(pltpu.roll(block, j, 1) for j in range(1, TAPS))
                terms = [w_ref[index * TAPS] * block]
                for j in range(1, TAPS):
                    shifted = jnp.where(lane >= j, rolled[j - 1], kept[j - 1])
                    terms.append(w_ref[index * TAPS + j] * shifted)
                total = summed(terms)
                kept = rolled
                feat_ref[index, s] = total
                if index == 0:
                    gate_ref[block_rows(s), :] = (raw_ref[3, s] * total).astype(bf16).astype(f32)
                if index == 2:
                    mix_ref[block_rows(s), :] = (feat_ref[1, s] * total).astype(bf16).astype(f32)
            return kept

        lax.fori_loop(0, blocks // 64, forward, (zero,) * (TAPS - 1))

    res_ref[...] = jnp.dot(gate_ref[...].astype(bf16), flip, preferred_element_type=f32)

    for b in range(GROUPS):
        for o in range(2):
            left_ref[o, b, : DEPTH * OWN, :] = jnp.zeros((DEPTH * OWN, LANES), f32)

    def lay(step, carry):
        carry = list(carry)
        for which in range(4):
            s = step * 4 + which
            sources = (mix_ref[block_rows(s), :], res_ref[block_rows(blocks - 1 - s), :])
            rows = pl.ds(pl.multiple_of((s + DEPTH) * OWN, OWN), OWN)
            for o, value in enumerate(sources):
                turns = (value,) + tuple(pltpu.roll(value, PIECE * k, 1) for k in range(1, GROUPS))
                history = (turns,) + carry[o]
                for b in range(GROUPS):
                    laid = history[0][-b % GROUPS]
                    for p in range(1, GROUPS):
                        laid = jnp.where(piece == p, history[p][(p - b) % GROUPS], laid)
                    left_ref[o, b, rows, :] = laid
                carry[o] = history[: GROUPS - 1]
        return tuple(carry)

    blank = ((zero,) * GROUPS,) * (GROUPS - 1)
    lax.fori_loop(0, steps, lay, (blank, blank), unroll=16)

    for r in range(OWN):
        for source, target in ((mix_ref, xm_ref), (tap_ref, xh_ref)):
            target[r] = source[pl.ds(r, blocks, stride=OWN), :]

    tile_row = lax.broadcasted_iota(jnp.int32, (PIECE, LANES), 0)
    tile_col = lax.broadcasted_iota(jnp.int32, (PIECE, LANES), 1)
    causal = tile_col >= tile_row
    full_row = lax.broadcasted_iota(jnp.int32, (blocks, LANES), 0)
    full_col = lax.broadcasted_iota(jnp.int32, (blocks, LANES), 1)
    reach = 4 * GROUPS

    def toeplitz(r, signal_ref, part, before):
        tiles = []
        for mu in range(part * reach, (part + 1) * reach):
            line = jnp.broadcast_to(signal_ref[r, mu : mu + 1, :], (PIECE, LANES))
            turned = pltpu.roll(line, 0, 1, stride=1, stride_axis=0)
            tiles.append(jnp.where(causal, turned, before).astype(bf16))
            before = turned
        return jnp.concatenate(tiles, axis=0), before

    def long_convs(r):
        before_taps = before_mix = jnp.zeros((PIECE, LANES), f32)
        for part in range(blocks // reach):
            taps, before_taps = toeplitz(r, xh_ref, part, before_taps)
            mix, before_mix = toeplitz(r, xm_ref, part, before_mix)
            start = part * reach
            height = blocks - start
            flat = (GROUPS * height, reach * PIECE)
            one = jnp.dot(lhs_ref[0, :, :height, :].reshape(flat), taps, preferred_element_type=f32)
            two = jnp.dot(
                lhs_ref[1, :, :height, :].reshape(flat),
                jnp.concatenate([taps, mix], axis=1),
                preferred_element_type=f32,
            )
            for o, product in enumerate((one, two[:, :LANES], two[:, LANES:])):
                product = product.reshape(GROUPS, height, LANES)
                if part == 0:
                    acc_ref[o] = product
                else:
                    acc_ref[o, :, start:, :] += product

    def gathered(o):
        total = acc_ref[o, 0]
        wrapped = jnp.zeros((blocks, LANES), f32)
        for b in range(1, GROUPS):
            moved = pltpu.roll(acc_ref[o, b], PIECE * b, 1)
            inside = full_col >= PIECE * b
            total = total + jnp.where(inside, moved, 0.0)
            wrapped = wrapped + jnp.where(inside, 0.0, moved)
        return total + jnp.where(full_row > 0, pltpu.roll(wrapped, 1, 0), 0.0)

    @pl.loop(0, OWN, unroll=4)
    def _(r):
        for o in range(2):
            for b in range(GROUPS):
                for depth in range(GROUPS):
                    rows = pl.ds((DEPTH - GROUPS * depth) * OWN + r, blocks, stride=OWN)
                    lanes = slice(depth * LANES, (depth + 1) * LANES)
                    lhs_ref[o, b, :, lanes] = left_ref[o, b, rows, :].astype(bf16)
        here = pl.ds(r, blocks, stride=OWN)
        long_convs(r)
        mix_ref[here, :] = gathered(0)
        gate_ref[here, :] = gathered(1)
        tap_ref[here, :] = gathered(2) * scale

    res_ref[...] = jnp.dot(gate_ref[...].astype(bf16), flip, preferred_element_type=f32)
    gate_ref[...] = jnp.dot(tap_ref[...].astype(bf16), flip, preferred_element_type=f32)

    def put(step, index, values):
        rows = jnp.concatenate(values, axis=0).astype(bf16).reshape(16, 2, LANES)
        out_ref[pl.ds(step * 16, 16), :, index * LANES : (index + 1) * LANES] = rows

    def back_block(s):
        return block_rows(blocks - 1 - s)

    @pl.loop(0, steps, unroll=16)
    def _(step):
        convs, mix_grads, taps_grad = [], [], []
        for which in range(4):
            s = step * 4 + which
            conv = mix_ref[block_rows(s), :].astype(bf16).astype(f32)
            mix_ref[block_rows(s), :] = conv
            convs.append(conv)
            mix_grads.append(res_ref[back_block(s), :])
            taps_grad.append(swap_pieces(gate_ref[back_block(s), :]))
        put(step, 0, convs)
        put(step, 1, mix_grads)
        put(step, 2, taps_grad)

    def grad_of(index, s):
        if index == 0:
            return raw_ref[3, s] * mix_ref[block_rows(s), :]
        return res_ref[back_block(s), :] * feat_ref[3 - index, s]

    all_sums = []
    for index in range(3):

        def backward(count, carry, index=index):
            kept, sums = carry
            for which in reversed(range(64)):
                s = (blocks // 64 - 1 - count) * 64 + which
                grad = grad_of(index, s)
                raw = raw_ref[index, s]
                rolled = tuple(pltpu.roll(grad, LANES - j, 1) for j in range(1, TAPS))
                new_sums = [sums[0] + raw * grad]
                for j in range(1, TAPS):
                    shifted = jnp.where(lane < LANES - j, rolled[j - 1], kept[j - 1])
                    new_sums.append(sums[j] + raw * shifted)
                kept, sums = rolled, tuple(new_sums)
            return kept, sums

        _, sums = lax.fori_loop(
            0, blocks // 64, backward, ((zero,) * (TAPS - 1), (zero,) * TAPS)
        )
        all_sums += sums

    high = zero
    low = zero
    for index, value in enumerate(all_sums):
        total = jnp.sum(value, axis=1, keepdims=True) * scale
        coarse = total.astype(bf16).astype(f32)
        high = jnp.where(lane == index, coarse, high)
        low = jnp.where(lane == index + 32, total - coarse, low)
    both = high + low
    octet = lane // OWN
    for step in range(steps):
        edges = []
        for s in range(step * 4, step * 4 + 4):
            edge = both
            for index in range(3):
                if s + 1 < blocks:
                    head = pltpu.roll(grad_of(index, s + 1), 64 + OWN * index, 1)
                    edge = jnp.where(octet == 8 + index, head, edge)
                if s > 0:
                    tail = pltpu.roll(raw_ref[index, s - 1], 96 + OWN + OWN * index, 1)
                    edge = jnp.where(octet == 12 + index, tail, edge)
            edges.append(edge)
        put(step, 3, edges)


def on_device(query_raw, key_raw, value_raw, featurizer, filter_taps, cotangent):
    tok_rows, channels = query_raw.shape
    blocks = lax.axis_size(SEQ)
    devices = lax.axis_size(SEQ_CH)
    small = pltpu.CompilerParams(vmem_limit_bytes=12 * MIB)
    large = pltpu.CompilerParams(vmem_limit_bytes=20 * MIB)
    me = lax.axis_index(SEQ_CH)
    sources = (query_raw, key_raw, value_raw, cotangent, filter_taps)

    packed = pl.pallas_call(
        pack_kernel,
        in_specs=[pl.BlockSpec(memory_space=pltpu.MemorySpace.HBM)] * len(sources),
        out_shape=jax.ShapeDtypeStruct((devices, 2, 5 * LANES), bf16),
        scratch_shapes=[pltpu.VMEM(source.shape, source.dtype) for source in sources]
        + [pltpu.SemaphoreType.DMA((len(sources),))],
        compiler_params=pltpu.CompilerParams(vmem_limit_bytes=60 * MIB),
        name="pack",
    )(*sources)
    received = lax.all_to_all(packed, SEQ_CH, split_axis=0, concat_axis=0, tiled=True)

    feat = jax.ShapeDtypeStruct((tok_rows, channels), f32)
    feats = pl.pallas_call(
        feat_kernel,
        out_shape=(feat,) * 3,
        scratch_shapes=[pltpu.VMEM((tok_rows + OWN, channels), f32)],
        compiler_params=small,
        cost_estimate=pl.CostEstimate(flops=3000000, bytes_accessed=1200000, transcendentals=0),
        name="feat",
    )(query_raw, key_raw, value_raw, featurizer)

    weights = lax.all_gather(featurizer, "ch")
    weights = lax.dynamic_slice(weights, (0, 0, 0, 2 * me), (GROUPS, 3, TAPS, 2))
    weights = weights.transpose(0, 3, 1, 2).reshape(OWN, 3 * TAPS)

    flat = pltpu.VMEM((blocks * OWN, LANES), f32)
    by_channel = pltpu.VMEM((OWN, blocks, LANES), f32)
    outgoing = pl.pallas_call(
        functools.partial(owner_kernel, blocks=blocks, scale=(blocks * LANES) ** -0.5),
        out_shape=jax.ShapeDtypeStruct((devices, 2, 4 * LANES), bf16),
        scratch_shapes=[
            pltpu.VMEM((3 * TAPS, OWN, LANES), f32),
            pltpu.VMEM((4, blocks, OWN, LANES), f32),
            pltpu.VMEM((3, blocks, OWN, LANES), f32),
            flat,
            flat,
            flat,
            by_channel,
            by_channel,
            flat,
            pltpu.VMEM((2, GROUPS, (blocks + DEPTH) * OWN, LANES), f32),
            pltpu.VMEM((2, GROUPS, blocks, GROUPS * LANES), bf16),
            pltpu.VMEM((3, GROUPS, blocks, LANES), f32),
        ],
        compiler_params=large,
        name="owner",
    )(received, weights)
    returned = lax.all_to_all(outgoing, SEQ_CH, split_axis=0, concat_axis=0, tiled=True)

    here = jax.ShapeDtypeStruct((tok_rows, channels), bf16)
    return pl.pallas_call(
        unpack_kernel,
        out_shape=(here,) * 4
        + (
            jax.ShapeDtypeStruct(filter_taps.shape, f32),
            jax.ShapeDtypeStruct(featurizer.shape, f32),
        ),
        scratch_shapes=[
            pltpu.VMEM((tok_rows, channels), f32),
            pltpu.VMEM((tok_rows, channels), f32),
            pltpu.VMEM((LANES + 2 * OWN, channels), f32),
            pltpu.VMEM((3, OWN, channels), f32),
            pltpu.VMEM((tok_rows + OWN, channels), f32),
        ],
        compiler_params=small,
        name="unpack",
    )(returned, *feats, cotangent, featurizer)


def solution(mesh):
    finer = Mesh(mesh.devices.reshape(2, 8, 4, mesh.shape["ch"]), ("seq_0", "seq_1", "seq_2", "ch"))
    placed = (
        P(SEQ, "ch"),
        P(SEQ, "ch"),
        P(SEQ, "ch"),
        P(None, None, "ch"),
        P(SEQ_CH, None),
        P(SEQ, "ch"),
    )
    return jax.shard_map(
        on_device,
        mesh=finer,
        in_specs=placed,
        out_specs=(
            P(SEQ, "ch"),
            P(SEQ, "ch"),
            P(SEQ, "ch"),
            P(SEQ, "ch"),
            P(SEQ_CH, None),
            P(None, None, "ch"),
        ),
        check_vma=False,
    )
```

```python
import functools

import jax
import jax.numpy as jnp
from jax import lax
from jax.experimental import pallas as pl
from jax.experimental.pallas import tpu as pltpu
from jax.sharding import Mesh
from jax.sharding import PartitionSpec as P

TAPS = 7
SEQ = ("seq_0", "seq_1", "seq_2")
SEQ_CH = ("seq_0", "seq_1", "seq_2", "ch")
LANES = 128
OWN = 8
GROUPS = 4
PIECE = LANES // GROUPS
DEPTH = 12
MIB = 1024 * 1024

f32 = jnp.float32
bf16 = jnp.bfloat16


def pack_kernel(*refs):
    sources, out_ref, copies, sems = refs[:5], refs[5], refs[6:11], refs[11]
    moves = [
        pltpu.make_async_copy(source, copy, sems.at[index])
        for index, (source, copy) in enumerate(zip(sources, copies))
    ]
    for move in moves:
        move.start()
    pairs = (out_ref.shape[0], 2, LANES)
    wide = out_ref.shape[0] * 2

    def put(index, rows):
        out_ref[:, :, index * LANES : (index + 1) * LANES] = rows.T.astype(bf16).reshape(pairs)

    for index in range(4):
        moves[index].wait()
        put(index, copies[index][...].astype(f32))
    moves[4].wait()
    taps = copies[4][...].astype(f32)
    put(4, jnp.concatenate([taps[:, g * wide : (g + 1) * wide] for g in range(GROUPS)], axis=0))


def feat_kernel(q_ref, k_ref, v_ref, w_ref, fq_ref, fk_ref, fv_ref, padded_ref):
    rows, wide = q_ref.shape
    padded_ref[:OWN, :] = jnp.zeros((OWN, wide), f32)
    for index, (ref, out_ref) in enumerate(((q_ref, fq_ref), (k_ref, fk_ref), (v_ref, fv_ref))):
        padded_ref[OWN:, :] = ref[...].astype(f32)
        for column in range(0, wide, LANES):
            part = slice(column, column + LANES)
            total = w_ref[index, 0:1, part] * padded_ref[OWN:, part]
            for j in range(1, TAPS):
                total = total + w_ref[index, j : j + 1, part] * padded_ref[OWN - j : OWN - j + rows, part]
            out_ref[:, part] = total


def unpack_kernel(
    in_ref,
    fq_ref,
    fk_ref,
    fv_ref,
    c_ref,
    w_ref,
    *refs,
):
    results, ready = refs[:6], refs[6:12]
    mixed_ref, qg_ref, kg_ref, vg_ref, fg_ref, wg_ref = ready
    conv_ref, grad_ref, edge_ref, first_ref, padded_ref, sems = refs[12:]
    wide = in_ref.shape[0] * 2
    rows = c_ref.shape[0]

    sends = []

    def send(index):
        sends.append(pltpu.make_async_copy(ready[index], results[index], sems.at[index]))
        sends[-1].start()

    def turned(index):
        values = in_ref[:, :, index * LANES : (index + 1) * LANES].reshape(wide, LANES)
        return values.astype(f32).T

    conv_ref[...] = turned(0)
    grad_ref[...] = turned(1)
    taps_grad = turned(2)
    for g in range(GROUPS):
        fg_ref[:, g * wide : (g + 1) * wide] = taps_grad[g * PIECE : (g + 1) * PIECE]
    send(4)
    edge_ref[:LANES, :] = turned(3)
    total = edge_ref[0:24, :] + edge_ref[32:56, :]
    for index in range(3):
        wg_ref[index] = total[TAPS * index : TAPS * (index + 1)]
    send(5)

    last = slice(LANES, LANES + OWN)
    after = slice(LANES + OWN, LANES + 2 * OWN)
    edge_ref[after, :] = jnp.zeros((OWN, wide), f32)
    for index, ref in enumerate((fq_ref, fk_ref, fv_ref)):
        edge_ref[last, :] = edge_ref[56 + 2 * OWN * index : 64 + 2 * OWN * index, :]
        first = ref[:OWN, :]
        for j in range(1, TAPS):
            start = LANES + OWN - j
            first = first + w_ref[index, j : j + 1, :] * edge_ref[start : start + OWN, :]
        first_ref[index] = first

    def feat(index, part):
        ref = (fq_ref, fk_ref, fv_ref)[index]
        return jnp.concatenate([first_ref[index, :, part], ref[OWN:, part]], axis=0)

    for index, out_ref in enumerate((qg_ref, kg_ref, vg_ref)):
        padded_ref[rows:, :] = edge_ref[64 + 2 * OWN * index : 72 + 2 * OWN * index, :]
        for column in range(0, wide, LANES):
            part = slice(column, column + LANES)
            if index == 0:
                conv = conv_ref[:, part]
                mixed_ref[:, part] = (feat(0, part) * conv).astype(bf16)
                grad = c_ref[:, part].astype(f32) * conv
            else:
                grad = grad_ref[:, part] * feat(3 - index, part)
            padded_ref[:rows, part] = grad
            total = w_ref[index, 0:1, part] * grad
            for j in range(1, TAPS):
                total = total + w_ref[index, j : j + 1, part] * padded_ref[j : j + rows, part]
            out_ref[:, part] = total.astype(bf16)
        if index == 0:
            send(0)
        send(index + 1)
    for one in sends:
        one.wait()


def owner_kernel(
    in_ref,
    own_ref,
    out_ref,
    w_ref,
    raw_ref,
    feat_ref,
    mix_ref,
    gate_ref,
    tap_ref,
    xm_ref,
    xh_ref,
    res_ref,
    left_ref,
    lhs_ref,
    acc_ref,
    *,
    blocks,
    scale,
):
    lane = lax.broadcasted_iota(jnp.int32, (OWN, LANES), 1)
    row = lax.broadcasted_iota(jnp.int32, (OWN, LANES), 0)
    group = row // 2
    piece = lane // PIECE
    flip_row = lax.broadcasted_iota(jnp.int32, (LANES, LANES), 0)
    flip_col = lax.broadcasted_iota(jnp.int32, (LANES, LANES), 1)
    flip = (flip_row + flip_col == LANES - 1).astype(f32).astype(bf16)
    zero = jnp.zeros((OWN, LANES), f32)
    steps = blocks // 4

    def swap_pieces(value):
        result = value
        for k in range(1, GROUPS):
            moved = pltpu.roll(pltpu.roll(value, PIECE * k, 1), OWN - 2 * k, 0)
            result = jnp.where(piece == (group + k) % GROUPS, moved, result)
        return result

    def summed(terms):
        while len(terms) > 1:
            pairs = [one + two for one, two in zip(terms[::2], terms[1::2])]
            terms = pairs + terms[len(pairs) * 2 :]
        return terms[0]

    def block_rows(s):
        return pl.ds(pl.multiple_of(s * OWN, OWN), OWN)

    def taken(step, index):
        rows = in_ref[pl.ds(step * 16, 16), :, index * LANES : (index + 1) * LANES]
        return rows.reshape(4 * OWN, LANES).astype(f32)

    for index in range(3 * TAPS):
        w_ref[index] = jnp.broadcast_to(own_ref[:, index : index + 1], (OWN, LANES))

    @pl.loop(0, steps, unroll=16)
    def _(step):
        for index in range(5):
            values = taken(step, index)
            for which in range(4):
                s = step * 4 + which
                value = values[which * OWN : (which + 1) * OWN]
                if index < 4:
                    raw_ref[index, s] = value
                else:
                    tap_ref[block_rows(s), :] = swap_pieces(value)

    for index in range(3):

        def forward(step, kept, index=index):
            for which in range(64):
                s = step * 64 + which
                block = raw_ref[index, s]
                rolled = tuple(pltpu.roll(block, j, 1) for j in range(1, TAPS))
                terms = [w_ref[index * TAPS] * block]
                for j in range(1, TAPS):
                    shifted = jnp.where(lane >= j, rolled[j - 1], kept[j - 1])
                    terms.append(w_ref[index * TAPS + j] * shifted)
                total = summed(terms)
                kept = rolled
                feat_ref[index, s] = total
                if index == 0:
                    gate_ref[block_rows(s), :] = (raw_ref[3, s] * total).astype(bf16).astype(f32)
                if index == 2:
                    mix_ref[block_rows(s), :] = (feat_ref[1, s] * total).astype(bf16).astype(f32)
            return kept

        lax.fori_loop(0, blocks // 64, forward, (zero,) * (TAPS - 1))

    res_ref[...] = jnp.dot(gate_ref[...].astype(bf16), flip, preferred_element_type=f32)

    for b in range(GROUPS):
        for o in range(2):
            left_ref[o, b, : DEPTH * OWN, :] = jnp.zeros((DEPTH * OWN, LANES), f32)

    def lay(step, carry):
        carry = list(carry)
        for which in range(4):
            s = step * 4 + which
            sources = (mix_ref[block_rows(s), :], res_ref[block_rows(blocks - 1 - s), :])
            rows = pl.ds(pl.multiple_of((s + DEPTH) * OWN, OWN), OWN)
            for o, value in enumerate(sources):
                turns = (value,) + tuple(pltpu.roll(value, PIECE * k, 1) for k in range(1, GROUPS))
                history = (turns,) + carry[o]
                for b in range(GROUPS):
                    laid = history[0][-b % GROUPS]
                    for p in range(1, GROUPS):
                        laid = jnp.where(piece == p, history[p][(p - b) % GROUPS], laid)
                    left_ref[o, b, rows, :] = laid
                carry[o] = history[: GROUPS - 1]
        return tuple(carry)

    blank = ((zero,) * GROUPS,) * (GROUPS - 1)
    lax.fori_loop(0, steps, lay, (blank, blank), unroll=16)

    for r in range(OWN):
        for source, target in ((mix_ref, xm_ref), (tap_ref, xh_ref)):
            target[r] = source[pl.ds(r, blocks, stride=OWN), :]

    tile_row = lax.broadcasted_iota(jnp.int32, (PIECE, LANES), 0)
    tile_col = lax.broadcasted_iota(jnp.int32, (PIECE, LANES), 1)
    causal = tile_col >= tile_row
    full_row = lax.broadcasted_iota(jnp.int32, (blocks, LANES), 0)
    full_col = lax.broadcasted_iota(jnp.int32, (blocks, LANES), 1)
    reach = 4 * GROUPS

    def toeplitz(r, signal_ref, part, before):
        tiles = []
        for mu in range(part * reach, (part + 1) * reach):
            line = jnp.broadcast_to(signal_ref[r, mu : mu + 1, :], (PIECE, LANES))
            turned = pltpu.roll(line, 0, 1, stride=1, stride_axis=0)
            tiles.append(jnp.where(causal, turned, before).astype(bf16))
            before = turned
        return jnp.concatenate(tiles, axis=0), before

    def long_convs(r):
        before_taps = before_mix = jnp.zeros((PIECE, LANES), f32)
        for part in range(blocks // reach):
            taps, before_taps = toeplitz(r, xh_ref, part, before_taps)
            mix, before_mix = toeplitz(r, xm_ref, part, before_mix)
            start = part * reach
            height = blocks - start
            flat = (GROUPS * height, reach * PIECE)
            one = jnp.dot(lhs_ref[0, :, :height, :].reshape(flat), taps, preferred_element_type=f32)
            two = jnp.dot(
                lhs_ref[1, :, :height, :].reshape(flat),
                jnp.concatenate([taps, mix], axis=1),
                preferred_element_type=f32,
            )
            for o, product in enumerate((one, two[:, :LANES], two[:, LANES:])):
                product = product.reshape(GROUPS, height, LANES)
                if part == 0:
                    acc_ref[o] = product
                else:
                    acc_ref[o, :, start:, :] += product

    def gathered(o):
        total = acc_ref[o, 0]
        wrapped = jnp.zeros((blocks, LANES), f32)
        for b in range(1, GROUPS):
            moved = pltpu.roll(acc_ref[o, b], PIECE * b, 1)
            inside = full_col >= PIECE * b
            total = total + jnp.where(inside, moved, 0.0)
            wrapped = wrapped + jnp.where(inside, 0.0, moved)
        return total + jnp.where(full_row > 0, pltpu.roll(wrapped, 1, 0), 0.0)

    @pl.loop(0, OWN, unroll=4)
    def _(r):
        for o in range(2):
            for b in range(GROUPS):
                for depth in range(GROUPS):
                    rows = pl.ds((DEPTH - GROUPS * depth) * OWN + r, blocks, stride=OWN)
                    lanes = slice(depth * LANES, (depth + 1) * LANES)
                    lhs_ref[o, b, :, lanes] = left_ref[o, b, rows, :].astype(bf16)
        here = pl.ds(r, blocks, stride=OWN)
        long_convs(r)
        mix_ref[here, :] = gathered(0)
        gate_ref[here, :] = gathered(1)
        tap_ref[here, :] = gathered(2) * scale

    res_ref[...] = jnp.dot(gate_ref[...].astype(bf16), flip, preferred_element_type=f32)
    gate_ref[...] = jnp.dot(tap_ref[...].astype(bf16), flip, preferred_element_type=f32)

    def put(step, index, values):
        rows = jnp.concatenate(values, axis=0).astype(bf16).reshape(16, 2, LANES)
        out_ref[pl.ds(step * 16, 16), :, index * LANES : (index + 1) * LANES] = rows

    def back_block(s):
        return block_rows(blocks - 1 - s)

    @pl.loop(0, steps, unroll=16)
    def _(step):
        convs, mix_grads, taps_grad = [], [], []
        for which in range(4):
            s = step * 4 + which
            conv = mix_ref[block_rows(s), :].astype(bf16).astype(f32)
            mix_ref[block_rows(s), :] = conv
            convs.append(conv)
            mix_grads.append(res_ref[back_block(s), :])
            taps_grad.append(swap_pieces(gate_ref[back_block(s), :]))
        put(step, 0, convs)
        put(step, 1, mix_grads)
        put(step, 2, taps_grad)

    def grad_of(index, s):
        if index == 0:
            return raw_ref[3, s] * mix_ref[block_rows(s), :]
        return res_ref[back_block(s), :] * feat_ref[3 - index, s]

    all_sums = []
    for index in range(3):

        def backward(count, carry, index=index):
            kept, sums = carry
            for which in reversed(range(64)):
                s = (blocks // 64 - 1 - count) * 64 + which
                grad = grad_of(index, s)
                raw = raw_ref[index, s]
                rolled = tuple(pltpu.roll(grad, LANES - j, 1) for j in range(1, TAPS))
                new_sums = [sums[0] + raw * grad]
                for j in range(1, TAPS):
                    shifted = jnp.where(lane < LANES - j, rolled[j - 1], kept[j - 1])
                    new_sums.append(sums[j] + raw * shifted)
                kept, sums = rolled, tuple(new_sums)
            return kept, sums

        _, sums = lax.fori_loop(
            0, blocks // 64, backward, ((zero,) * (TAPS - 1), (zero,) * TAPS)
        )
        all_sums += sums

    high = zero
    low = zero
    for index, value in enumerate(all_sums):
        total = jnp.sum(value, axis=1, keepdims=True) * scale
        coarse = total.astype(bf16).astype(f32)
        high = jnp.where(lane == index, coarse, high)
        low = jnp.where(lane == index + 32, total - coarse, low)
    both = high + low
    last_octet = lane >= LANES - OWN
    for step in range(steps):
        edges = []
        for s in range(step * 4, step * 4 + 4):
            edge = both
            for index in range(3):
                head = grad_of(index, s + 1) if s + 1 < blocks else zero
                tail = raw_ref[index, s - 1] if s > 0 else zero
                ends = pltpu.roll(jnp.where(last_octet, tail, head), 64 + 2 * OWN * index, 1)
                edge = jnp.where((lane + OWN) // (2 * OWN) == 4 + index, ends, edge)
            edges.append(edge)
        put(step, 3, edges)


def on_device(query_raw, key_raw, value_raw, featurizer, filter_taps, cotangent):
    tok_rows, channels = query_raw.shape
    blocks = lax.axis_size(SEQ)
    devices = lax.axis_size(SEQ_CH)
    small = pltpu.CompilerParams(vmem_limit_bytes=12 * MIB)
    large = pltpu.CompilerParams(vmem_limit_bytes=20 * MIB)
    me = lax.axis_index(SEQ_CH)
    sources = (query_raw, key_raw, value_raw, cotangent, filter_taps)

    packed = pl.pallas_call(
        pack_kernel,
        in_specs=[pl.BlockSpec(memory_space=pltpu.MemorySpace.HBM)] * len(sources),
        out_shape=jax.ShapeDtypeStruct((devices, 2, 5 * LANES), bf16),
        scratch_shapes=[pltpu.VMEM(source.shape, source.dtype) for source in sources]
        + [pltpu.SemaphoreType.DMA((len(sources),))],
        compiler_params=pltpu.CompilerParams(vmem_limit_bytes=60 * MIB),
        name="pack",
    )(*sources)
    received = lax.all_to_all(packed, SEQ_CH, split_axis=0, concat_axis=0, tiled=True)

    feat = jax.ShapeDtypeStruct((tok_rows, channels), f32)
    feats = pl.pallas_call(
        feat_kernel,
        out_shape=(feat,) * 3,
        scratch_shapes=[pltpu.VMEM((tok_rows + OWN, channels), f32)],
        compiler_params=small,
        cost_estimate=pl.CostEstimate(flops=3000000, bytes_accessed=1200000, transcendentals=0),
        name="feat",
    )(query_raw, key_raw, value_raw, featurizer)

    weights = lax.all_gather(featurizer, "ch")
    weights = lax.dynamic_slice(weights, (0, 0, 0, 2 * me), (GROUPS, 3, TAPS, 2))
    weights = weights.transpose(0, 3, 1, 2).reshape(OWN, 3 * TAPS)

    flat = pltpu.VMEM((blocks * OWN, LANES), f32)
    by_channel = pltpu.VMEM((OWN, blocks, LANES), f32)
    outgoing = pl.pallas_call(
        functools.partial(owner_kernel, blocks=blocks, scale=(blocks * LANES) ** -0.5),
        out_shape=jax.ShapeDtypeStruct((devices, 2, 4 * LANES), bf16),
        scratch_shapes=[
            pltpu.VMEM((3 * TAPS, OWN, LANES), f32),
            pltpu.VMEM((4, blocks, OWN, LANES), f32),
            pltpu.VMEM((3, blocks, OWN, LANES), f32),
            flat,
            flat,
            flat,
            by_channel,
            by_channel,
            flat,
            pltpu.VMEM((2, GROUPS, (blocks + DEPTH) * OWN, LANES), f32),
            pltpu.VMEM((2, GROUPS, blocks, GROUPS * LANES), bf16),
            pltpu.VMEM((3, GROUPS, blocks, LANES), f32),
        ],
        compiler_params=large,
        name="owner",
    )(received, weights)
    returned = lax.all_to_all(outgoing, SEQ_CH, split_axis=0, concat_axis=0, tiled=True)

    here = jax.ShapeDtypeStruct((tok_rows, channels), bf16)
    results = (here,) * 4 + (
        jax.ShapeDtypeStruct(filter_taps.shape, f32),
        jax.ShapeDtypeStruct(featurizer.shape, f32),
    )
    return pl.pallas_call(
        unpack_kernel,
        out_specs=[pl.BlockSpec(memory_space=pltpu.MemorySpace.HBM)] * len(results),
        out_shape=results,
        scratch_shapes=[pltpu.VMEM(result.shape, result.dtype) for result in results]
        + [
            pltpu.VMEM((tok_rows, channels), f32),
            pltpu.VMEM((tok_rows, channels), f32),
            pltpu.VMEM((LANES + 2 * OWN, channels), f32),
            pltpu.VMEM((3, OWN, channels), f32),
            pltpu.VMEM((tok_rows + OWN, channels), f32),
            pltpu.SemaphoreType.DMA((len(results),)),
        ],
        compiler_params=small,
        name="unpack",
    )(returned, *feats, cotangent, featurizer)


def solution(mesh):
    finer = Mesh(mesh.devices.reshape(2, 8, 4, mesh.shape["ch"]), ("seq_0", "seq_1", "seq_2", "ch"))
    placed = (
        P(SEQ, "ch"),
        P(SEQ, "ch"),
        P(SEQ, "ch"),
        P(None, None, "ch"),
        P(SEQ_CH, None),
        P(SEQ, "ch"),
    )
    return jax.shard_map(
        on_device,
        mesh=finer,
        in_specs=placed,
        out_specs=(
            P(SEQ, "ch"),
            P(SEQ, "ch"),
            P(SEQ, "ch"),
            P(SEQ, "ch"),
            P(SEQ_CH, None),
            P(None, None, "ch"),
        ),
        check_vma=False,
    )
```

```python
import functools

import jax
import jax.numpy as jnp
from jax import lax
from jax.experimental import pallas as pl
from jax.experimental.pallas import tpu as pltpu
from jax.sharding import Mesh
from jax.sharding import PartitionSpec as P

TAPS = 7
SEQ = ("seq_0", "seq_1", "seq_2")
SEQ_CH = ("seq_0", "seq_1", "seq_2", "ch")
LANES = 128
OWN = 8
GROUPS = 4
PIECE = LANES // GROUPS
DEPTH = 12
MIB = 1024 * 1024

f32 = jnp.float32
bf16 = jnp.bfloat16


def pack_kernel(*refs):
    sources, out_ref, copies, sems = refs[:5], refs[5], refs[6:11], refs[11]
    ready_ref, sent_sems = refs[12:]
    moves = [
        pltpu.make_async_copy(source, copy, sems.at[index])
        for index, (source, copy) in enumerate(zip(sources, copies))
    ]
    for move in moves:
        move.start()
    pairs = (out_ref.shape[0], 2, LANES)
    wide = out_ref.shape[0] * 2

    sends = []

    def put(index, rows):
        ready_ref[index] = rows.T.astype(bf16).reshape(pairs)
        place = out_ref.at[:, :, index * LANES : (index + 1) * LANES]
        sends.append(pltpu.make_async_copy(ready_ref.at[index], place, sent_sems.at[index]))
        sends[index].start()

    for index in range(4):
        moves[index].wait()
        put(index, copies[index][...].astype(f32))
    moves[4].wait()
    taps = copies[4][...].astype(f32)
    put(4, jnp.concatenate([taps[:, g * wide : (g + 1) * wide] for g in range(GROUPS)], axis=0))
    for send in sends:
        send.wait()


def feat_kernel(q_ref, k_ref, v_ref, w_ref, fq_ref, fk_ref, fv_ref, padded_ref):
    rows, wide = q_ref.shape
    padded_ref[:OWN, :] = jnp.zeros((OWN, wide), f32)
    for index, (ref, out_ref) in enumerate(((q_ref, fq_ref), (k_ref, fk_ref), (v_ref, fv_ref))):
        padded_ref[OWN:, :] = ref[...].astype(f32)
        for column in range(0, wide, LANES):
            part = slice(column, column + LANES)
            total = w_ref[index, 0:1, part] * padded_ref[OWN:, part]
            for j in range(1, TAPS):
                total = total + w_ref[index, j : j + 1, part] * padded_ref[OWN - j : OWN - j + rows, part]
            out_ref[:, part] = total


def unpack_kernel(
    in_ref,
    fq_ref,
    fk_ref,
    fv_ref,
    c_ref,
    w_ref,
    *refs,
):
    results, ready = refs[:6], refs[6:12]
    mixed_ref, qg_ref, kg_ref, vg_ref, fg_ref, wg_ref = ready
    conv_ref, grad_ref, edge_ref, first_ref, padded_ref, sems = refs[12:]
    wide = in_ref.shape[0] * 2
    rows = c_ref.shape[0]

    sends = []

    def send(index):
        sends.append(pltpu.make_async_copy(ready[index], results[index], sems.at[index]))
        sends[-1].start()

    def turned(index):
        values = in_ref[:, :, index * LANES : (index + 1) * LANES].reshape(wide, LANES)
        return values.astype(f32).T

    conv_ref[...] = turned(0)
    grad_ref[...] = turned(1)
    taps_grad = turned(2)
    for g in range(GROUPS):
        fg_ref[:, g * wide : (g + 1) * wide] = taps_grad[g * PIECE : (g + 1) * PIECE]
    send(4)
    edge_ref[:LANES, :] = turned(3)
    total = edge_ref[0:24, :] + edge_ref[32:56, :]
    for index in range(3):
        wg_ref[index] = total[TAPS * index : TAPS * (index + 1)]
    send(5)

    last = slice(LANES, LANES + OWN)
    after = slice(LANES + OWN, LANES + 2 * OWN)
    edge_ref[after, :] = jnp.zeros((OWN, wide), f32)
    for index, ref in enumerate((fq_ref, fk_ref, fv_ref)):
        edge_ref[last, :] = edge_ref[56 + 2 * OWN * index : 64 + 2 * OWN * index, :]
        first = ref[:OWN, :]
        for j in range(1, TAPS):
            start = LANES + OWN - j
            first = first + w_ref[index, j : j + 1, :] * edge_ref[start : start + OWN, :]
        first_ref[index] = first

    def feat(index, part):
        ref = (fq_ref, fk_ref, fv_ref)[index]
        return jnp.concatenate([first_ref[index, :, part], ref[OWN:, part]], axis=0)

    for index, out_ref in enumerate((qg_ref, kg_ref, vg_ref)):
        padded_ref[rows:, :] = edge_ref[64 + 2 * OWN * index : 72 + 2 * OWN * index, :]
        for column in range(0, wide, LANES):
            part = slice(column, column + LANES)
            if index == 0:
                conv = conv_ref[:, part]
                mixed_ref[:, part] = (feat(0, part) * conv).astype(bf16)
                grad = c_ref[:, part].astype(f32) * conv
            else:
                grad = grad_ref[:, part] * feat(3 - index, part)
            padded_ref[:rows, part] = grad
            total = w_ref[index, 0:1, part] * grad
            for j in range(1, TAPS):
                total = total + w_ref[index, j : j + 1, part] * padded_ref[j : j + rows, part]
            out_ref[:, part] = total.astype(bf16)
        if index == 0:
            send(0)
        send(index + 1)
    for one in sends:
        one.wait()


def owner_kernel(
    in_ref,
    own_ref,
    out_ref,
    w_ref,
    raw_ref,
    feat_ref,
    mix_ref,
    gate_ref,
    tap_ref,
    xm_ref,
    xh_ref,
    res_ref,
    left_ref,
    lhs_ref,
    acc_ref,
    *,
    blocks,
    scale,
):
    lane = lax.broadcasted_iota(jnp.int32, (OWN, LANES), 1)
    row = lax.broadcasted_iota(jnp.int32, (OWN, LANES), 0)
    group = row // 2
    piece = lane // PIECE
    flip_row = lax.broadcasted_iota(jnp.int32, (LANES, LANES), 0)
    flip_col = lax.broadcasted_iota(jnp.int32, (LANES, LANES), 1)
    flip = (flip_row + flip_col == LANES - 1).astype(f32).astype(bf16)
    zero = jnp.zeros((OWN, LANES), f32)
    steps = blocks // 4

    def swap_pieces(value):
        result = value
        for k in range(1, GROUPS):
            moved = pltpu.roll(pltpu.roll(value, PIECE * k, 1), OWN - 2 * k, 0)
            result = jnp.where(piece == (group + k) % GROUPS, moved, result)
        return result

    def summed(terms):
        while len(terms) > 1:
            pairs = [one + two for one, two in zip(terms[::2], terms[1::2])]
            terms = pairs + terms[len(pairs) * 2 :]
        return terms[0]

    def block_rows(s):
        return pl.ds(pl.multiple_of(s * OWN, OWN), OWN)

    def taken(step, index):
        rows = in_ref[pl.ds(step * 16, 16), :, index * LANES : (index + 1) * LANES]
        return rows.reshape(4 * OWN, LANES).astype(f32)

    for index in range(3 * TAPS):
        w_ref[index] = jnp.broadcast_to(own_ref[:, index : index + 1], (OWN, LANES))

    @pl.loop(0, steps, unroll=16)
    def _(step):
        for index in range(5):
            values = taken(step, index)
            for which in range(4):
                s = step * 4 + which
                value = values[which * OWN : (which + 1) * OWN]
                if index < 4:
                    raw_ref[index, s] = value
                else:
                    tap_ref[block_rows(s), :] = swap_pieces(value)

    for index in range(3):

        def forward(step, kept, index=index):
            for which in range(64):
                s = step * 64 + which
                block = raw_ref[index, s]
                rolled = tuple(pltpu.roll(block, j, 1) for j in range(1, TAPS))
                terms = [w_ref[index * TAPS] * block]
                for j in range(1, TAPS):
                    shifted = jnp.where(lane >= j, rolled[j - 1], kept[j - 1])
                    terms.append(w_ref[index * TAPS + j] * shifted)
                total = summed(terms)
                kept = rolled
                feat_ref[index, s] = total
                if index == 0:
                    gate_ref[block_rows(s), :] = (raw_ref[3, s] * total).astype(bf16).astype(f32)
                if index == 2:
                    mix_ref[block_rows(s), :] = (feat_ref[1, s] * total).astype(bf16).astype(f32)
            return kept

        lax.fori_loop(0, blocks // 64, forward, (zero,) * (TAPS - 1))

    res_ref[...] = jnp.dot(gate_ref[...].astype(bf16), flip, preferred_element_type=f32)

    for b in range(GROUPS):
        for o in range(2):
            left_ref[o, b, : DEPTH * OWN, :] = jnp.zeros((DEPTH * OWN, LANES), f32)

    def lay(step, carry):
        carry = list(carry)
        for which in range(4):
            s = step * 4 + which
            sources = (mix_ref[block_rows(s), :], res_ref[block_rows(blocks - 1 - s), :])
            rows = pl.ds(pl.multiple_of((s + DEPTH) * OWN, OWN), OWN)
            for o, value in enumerate(sources):
                turns = (value,) + tuple(pltpu.roll(value, PIECE * k, 1) for k in range(1, GROUPS))
                history = (turns,) + carry[o]
                for b in range(GROUPS):
                    laid = history[0][-b % GROUPS]
                    for p in range(1, GROUPS):
                        laid = jnp.where(piece == p, history[p][(p - b) % GROUPS], laid)
                    left_ref[o, b, rows, :] = laid
                carry[o] = history[: GROUPS - 1]
        return tuple(carry)

    blank = ((zero,) * GROUPS,) * (GROUPS - 1)
    lax.fori_loop(0, steps, lay, (blank, blank), unroll=16)

    for r in range(OWN):
        for source, target in ((mix_ref, xm_ref), (tap_ref, xh_ref)):
            target[r] = source[pl.ds(r, blocks, stride=OWN), :]

    tile_row = lax.broadcasted_iota(jnp.int32, (PIECE, LANES), 0)
    tile_col = lax.broadcasted_iota(jnp.int32, (PIECE, LANES), 1)
    causal = tile_col >= tile_row
    full_row = lax.broadcasted_iota(jnp.int32, (blocks, LANES), 0)
    full_col = lax.broadcasted_iota(jnp.int32, (blocks, LANES), 1)
    reach = 4 * GROUPS

    def toeplitz(r, signal_ref, part, before):
        tiles = []
        for mu in range(part * reach, (part + 1) * reach):
            line = jnp.broadcast_to(signal_ref[r, mu : mu + 1, :], (PIECE, LANES))
            turned = pltpu.roll(line, 0, 1, stride=1, stride_axis=0)
            tiles.append(jnp.where(causal, turned, before).astype(bf16))
            before = turned
        return jnp.concatenate(tiles, axis=0), before

    def long_convs(r):
        before_taps = before_mix = jnp.zeros((PIECE, LANES), f32)
        for part in range(blocks // reach):
            taps, before_taps = toeplitz(r, xh_ref, part, before_taps)
            mix, before_mix = toeplitz(r, xm_ref, part, before_mix)
            start = part * reach
            height = blocks - start
            flat = (GROUPS * height, reach * PIECE)
            one = jnp.dot(lhs_ref[0, :, :height, :].reshape(flat), taps, preferred_element_type=f32)
            two = jnp.dot(
                lhs_ref[1, :, :height, :].reshape(flat),
                jnp.concatenate([taps, mix], axis=1),
                preferred_element_type=f32,
            )
            for o, product in enumerate((one, two[:, :LANES], two[:, LANES:])):
                product = product.reshape(GROUPS, height, LANES)
                if part == 0:
                    acc_ref[o] = product
                else:
                    acc_ref[o, :, start:, :] += product

    def gathered(o):
        total = acc_ref[o, 0]
        wrapped = jnp.zeros((blocks, LANES), f32)
        for b in range(1, GROUPS):
            moved = pltpu.roll(acc_ref[o, b], PIECE * b, 1)
            inside = full_col >= PIECE * b
            total = total + jnp.where(inside, moved, 0.0)
            wrapped = wrapped + jnp.where(inside, 0.0, moved)
        return total + jnp.where(full_row > 0, pltpu.roll(wrapped, 1, 0), 0.0)

    @pl.loop(0, OWN, unroll=4)
    def _(r):
        for o in range(2):
            for b in range(GROUPS):
                for depth in range(GROUPS):
                    rows = pl.ds((DEPTH - GROUPS * depth) * OWN + r, blocks, stride=OWN)
                    lanes = slice(depth * LANES, (depth + 1) * LANES)
                    lhs_ref[o, b, :, lanes] = left_ref[o, b, rows, :].astype(bf16)
        here = pl.ds(r, blocks, stride=OWN)
        long_convs(r)
        mix_ref[here, :] = gathered(0)
        gate_ref[here, :] = gathered(1)
        tap_ref[here, :] = gathered(2) * scale

    res_ref[...] = jnp.dot(gate_ref[...].astype(bf16), flip, preferred_element_type=f32)
    gate_ref[...] = jnp.dot(tap_ref[...].astype(bf16), flip, preferred_element_type=f32)

    def put(step, index, values):
        rows = jnp.concatenate(values, axis=0).astype(bf16).reshape(16, 2, LANES)
        out_ref[pl.ds(step * 16, 16), :, index * LANES : (index + 1) * LANES] = rows

    def back_block(s):
        return block_rows(blocks - 1 - s)

    @pl.loop(0, steps, unroll=16)
    def _(step):
        convs, mix_grads, taps_grad = [], [], []
        for which in range(4):
            s = step * 4 + which
            conv = mix_ref[block_rows(s), :].astype(bf16).astype(f32)
            mix_ref[block_rows(s), :] = conv
            convs.append(conv)
            mix_grads.append(res_ref[back_block(s), :])
            taps_grad.append(swap_pieces(gate_ref[back_block(s), :]))
        put(step, 0, convs)
        put(step, 1, mix_grads)
        put(step, 2, taps_grad)

    def grad_of(index, s):
        if index == 0:
            return raw_ref[3, s] * mix_ref[block_rows(s), :]
        return res_ref[back_block(s), :] * feat_ref[3 - index, s]

    all_sums = []
    for index in range(3):

        def backward(count, carry, index=index):
            kept, sums = carry
            for which in reversed(range(64)):
                s = (blocks // 64 - 1 - count) * 64 + which
                grad = grad_of(index, s)
                raw = raw_ref[index, s]
                rolled = tuple(pltpu.roll(grad, LANES - j, 1) for j in range(1, TAPS))
                new_sums = [sums[0] + raw * grad]
                for j in range(1, TAPS):
                    shifted = jnp.where(lane < LANES - j, rolled[j - 1], kept[j - 1])
                    new_sums.append(sums[j] + raw * shifted)
                kept, sums = rolled, tuple(new_sums)
            return kept, sums

        _, sums = lax.fori_loop(
            0, blocks // 64, backward, ((zero,) * (TAPS - 1), (zero,) * TAPS)
        )
        all_sums += sums

    high = zero
    low = zero
    for index, value in enumerate(all_sums):
        total = jnp.sum(value, axis=1, keepdims=True) * scale
        coarse = total.astype(bf16).astype(f32)
        high = jnp.where(lane == index, coarse, high)
        low = jnp.where(lane == index + 32, total - coarse, low)
    both = high + low
    last_octet = lane >= LANES - OWN
    for step in range(steps):
        edges = []
        for s in range(step * 4, step * 4 + 4):
            edge = both
            for index in range(3):
                head = grad_of(index, s + 1) if s + 1 < blocks else zero
                tail = raw_ref[index, s - 1] if s > 0 else zero
                ends = pltpu.roll(jnp.where(last_octet, tail, head), 64 + 2 * OWN * index, 1)
                edge = jnp.where((lane + OWN) // (2 * OWN) == 4 + index, ends, edge)
            edges.append(edge)
        put(step, 3, edges)


def on_device(query_raw, key_raw, value_raw, featurizer, filter_taps, cotangent):
    tok_rows, channels = query_raw.shape
    blocks = lax.axis_size(SEQ)
    devices = lax.axis_size(SEQ_CH)
    small = pltpu.CompilerParams(vmem_limit_bytes=12 * MIB)
    large = pltpu.CompilerParams(vmem_limit_bytes=20 * MIB)
    me = lax.axis_index(SEQ_CH)
    sources = (query_raw, key_raw, value_raw, cotangent, filter_taps)

    packed = pl.pallas_call(
        pack_kernel,
        in_specs=[pl.BlockSpec(memory_space=pltpu.MemorySpace.HBM)] * len(sources),
        out_specs=pl.BlockSpec(memory_space=pltpu.MemorySpace.HBM),
        out_shape=jax.ShapeDtypeStruct((devices, 2, 5 * LANES), bf16),
        scratch_shapes=[pltpu.VMEM(source.shape, source.dtype) for source in sources]
        + [
            pltpu.SemaphoreType.DMA((len(sources),)),
            pltpu.VMEM((len(sources), devices, 2, LANES), bf16),
            pltpu.SemaphoreType.DMA((len(sources),)),
        ],
        compiler_params=pltpu.CompilerParams(vmem_limit_bytes=60 * MIB),
        name="pack",
    )(*sources)
    received = lax.all_to_all(packed, SEQ_CH, split_axis=0, concat_axis=0, tiled=True)

    feat = jax.ShapeDtypeStruct((tok_rows, channels), f32)
    feats = pl.pallas_call(
        feat_kernel,
        out_shape=(feat,) * 3,
        scratch_shapes=[pltpu.VMEM((tok_rows + OWN, channels), f32)],
        compiler_params=small,
        cost_estimate=pl.CostEstimate(flops=3000000, bytes_accessed=1200000, transcendentals=0),
        name="feat",
    )(query_raw, key_raw, value_raw, featurizer)

    weights = lax.all_gather(featurizer, "ch")
    weights = lax.dynamic_slice(weights, (0, 0, 0, 2 * me), (GROUPS, 3, TAPS, 2))
    weights = weights.transpose(0, 3, 1, 2).reshape(OWN, 3 * TAPS)

    flat = pltpu.VMEM((blocks * OWN, LANES), f32)
    by_channel = pltpu.VMEM((OWN, blocks, LANES), f32)
    outgoing = pl.pallas_call(
        functools.partial(owner_kernel, blocks=blocks, scale=(blocks * LANES) ** -0.5),
        out_shape=jax.ShapeDtypeStruct((devices, 2, 4 * LANES), bf16),
        scratch_shapes=[
            pltpu.VMEM((3 * TAPS, OWN, LANES), f32),
            pltpu.VMEM((4, blocks, OWN, LANES), f32),
            pltpu.VMEM((3, blocks, OWN, LANES), f32),
            flat,
            flat,
            flat,
            by_channel,
            by_channel,
            flat,
            pltpu.VMEM((2, GROUPS, (blocks + DEPTH) * OWN, LANES), f32),
            pltpu.VMEM((2, GROUPS, blocks, GROUPS * LANES), bf16),
            pltpu.VMEM((3, GROUPS, blocks, LANES), f32),
        ],
        compiler_params=large,
        name="owner",
    )(received, weights)
    returned = lax.all_to_all(outgoing, SEQ_CH, split_axis=0, concat_axis=0, tiled=True)

    here = jax.ShapeDtypeStruct((tok_rows, channels), bf16)
    results = (here,) * 4 + (
        jax.ShapeDtypeStruct(filter_taps.shape, f32),
        jax.ShapeDtypeStruct(featurizer.shape, f32),
    )
    return pl.pallas_call(
        unpack_kernel,
        out_specs=[pl.BlockSpec(memory_space=pltpu.MemorySpace.HBM)] * len(results),
        out_shape=results,
        scratch_shapes=[pltpu.VMEM(result.shape, result.dtype) for result in results]
        + [
            pltpu.VMEM((tok_rows, channels), f32),
            pltpu.VMEM((tok_rows, channels), f32),
            pltpu.VMEM((LANES + 2 * OWN, channels), f32),
            pltpu.VMEM((3, OWN, channels), f32),
            pltpu.VMEM((tok_rows + OWN, channels), f32),
            pltpu.SemaphoreType.DMA((len(results),)),
        ],
        compiler_params=small,
        name="unpack",
    )(returned, *feats, cotangent, featurizer)


def solution(mesh):
    finer = Mesh(mesh.devices.reshape(2, 8, 4, mesh.shape["ch"]), ("seq_0", "seq_1", "seq_2", "ch"))
    placed = (
        P(SEQ, "ch"),
        P(SEQ, "ch"),
        P(SEQ, "ch"),
        P(None, None, "ch"),
        P(SEQ_CH, None),
        P(SEQ, "ch"),
    )
    return jax.shard_map(
        on_device,
        mesh=finer,
        in_specs=placed,
        out_specs=(
            P(SEQ, "ch"),
            P(SEQ, "ch"),
            P(SEQ, "ch"),
            P(SEQ, "ch"),
            P(SEQ_CH, None),
            P(None, None, "ch"),
        ),
        check_vma=False,
    )
```
